32 devices in a mesh: sub: 16 (over z, y, x), node: 2 (over core).
Axes of the slice: x: 2, y: 2, z: 4, core: 2. Of those that a mesh axis runs over, the one named last changes fastest.
Arguments:
- search_vectors: float32 [16384, 256], P('sub'), may hold values from -60 to 60
- ritz_values: float32 [256], replicated, may hold values from -0.9 to 0.9
- matrix_blocks: float32 [128, 4, 128, 128], P('sub'), may hold values from -0.25 to 0.25
- block_lists: int32 [128, 4], P('sub'), may hold values from 0 to 127, as said below
- inverses: float32 [4, 2, 128, 128, 128], P('node', None, 'sub'), may hold values from -0.5 to 0.5
- panels: float32 [16, 512, 1024], P('sub'), may hold values from -0.1875 to 0.1875
- separator_map: int32 [16, 4], P('sub'), may hold values from 0 to 7, as said below
- separator_shift: float32 [1024], replicated, may hold values from -0.9 to 0.9
Outputs:
- normalized_vectors: float32 [16384, 256], P('sub', 'node')
The draws below stay inside these ranges and needn't reach their ends.
Inputs may be any that keep to these rules, and one draw needn't show every extreme that they name: `block_lists`: entry 0 of row g is g; the other entries of row g are distinct blocks from g - 4 to g + 4, none equal to g. `separator_map`: the entries of one row are distinct.
All inputs are finite; a program needn't handle non-finite values.
Results may differ from the reference program's by a relative error of at most 0.0001.
Values sent between devices are 32-bit elements; how exact they have to be, the bound alone decides.
A program may use at most 64 MiB of HBM per device.

```python
import math
import jax
import jax.numpy as jnp
from jax import lax

VECS = 256
BLK = 128
ROWS = 1024
DEGREE = 4
HALO_BLOCKS = 4
SEP = 512
SEP_GROUPS = 8
NODES = 4
SUBS = 16
NROWS = 16384
NBLK = 8
BLOCKS = 128
SEP_BLOCKS = 4
GSEP = 1024


def draw_search_vectors(key, part):
    positions = jnp.arange(NROWS, dtype=jnp.float32) / max(NROWS - 1, 1)
    row_scale = jnp.exp(jnp.log(3.0) * positions)[:, None]
    values = jax.random.normal(jax.random.fold_in(key, 24), (NROWS, VECS), jnp.float32) * row_scale
    return jnp.clip(values, -60.0, 60.0)


def draw_block_lists(key, part):
    random_bits = jax.random.randint(jax.random.fold_in(key, 31), (BLOCKS, 2 * HALO_BLOCKS), 0, 2 ** 20, dtype=jnp.int32)
    offsets = jnp.concatenate([jnp.arange(-HALO_BLOCKS, 0, dtype=jnp.int32), jnp.arange(1, HALO_BLOCKS + 1, dtype=jnp.int32)])
    own_block = jnp.arange(BLOCKS, dtype=jnp.int32)[:, None]
    targets = own_block + offsets[None, :]
    valid = ((targets >= 0) & (targets < BLOCKS)).astype(jnp.int32)
    scores = random_bits * (2 * HALO_BLOCKS) + jnp.arange(2 * HALO_BLOCKS, dtype=jnp.int32)[None, :] + valid * 2 ** 26
    chosen_idx = lax.top_k(scores, DEGREE - 1)[1]
    chosen = jnp.take_along_axis(targets, chosen_idx, axis=1)
    return jnp.concatenate([own_block, chosen], axis=1).astype(jnp.int32)


def draw_separator_map(key, part):
    random_bits = jax.random.randint(jax.random.fold_in(key, 41), (SUBS, SEP_GROUPS), 0, 2 ** 20, dtype=jnp.int32)
    scores = random_bits * SEP_GROUPS + jnp.arange(SEP_GROUPS, dtype=jnp.int32)[None, :]
    return lax.top_k(scores, SEP_BLOCKS)[1].astype(jnp.int32)


def levels(stream_key, shape, pieces, least, largest):
    loudness = 1.0
    for position, shards_of in pieces:
        steps = jax.random.uniform(jax.random.fold_in(jax.random.fold_in(stream_key, 6), position), (shards_of,), jnp.float32, least / len(pieces), largest / len(pieces))
        loudness = loudness * jnp.repeat(jnp.exp(steps), shape[position] // shards_of).reshape((-1,) + (1,) * (len(shape) - 1 - position))
    return loudness


def noise(rng, dims, width, reach, cuts=(), kind=jnp.bfloat16):
    array = jax.random.normal(rng, dims, jnp.float32) * width
    if len(cuts) > 0:
        array = levels(rng, dims, cuts, -0.22, 0.18) * array
    return jnp.clip(array, min=-reach, max=reach).astype(kind)


def setup_inputs(seed: int = 0) -> dict:
    splits = jax.random.split(jax.random.key(seed), 9)
    search_vectors = draw_search_vectors(jax.random.fold_in(splits[8], 71), 0)
    ritz_values = jnp.clip(jax.random.uniform(splits[1], (VECS,), jnp.float32, -0.9, 0.9), -0.9, 0.9)
    matrix_blocks = noise(splits[2], (BLOCKS, DEGREE, BLK, BLK), (DEGREE * BLK) ** -0.5, 0.25, ((0, 16),), jnp.float32)
    block_lists = draw_block_lists(jax.random.fold_in(splits[8], 71), 0)
    inverses = noise(splits[4], (NODES, 2, BLOCKS, BLK, BLK), BLK ** -0.5, 0.5, ((0, 2), (2, 16)), jnp.float32)
    panels = noise(splits[5], (SUBS, SEP, ROWS), ROWS ** -0.5, 0.1875, ((0, 16),), jnp.float32)
    separator_map = draw_separator_map(jax.random.fold_in(splits[8], 71), 0)
    separator_shift = jnp.clip(jax.random.uniform(splits[7], (GSEP,), jnp.float32, -0.9, 0.9), -0.9, 0.9)
    return dict(search_vectors=search_vectors, ritz_values=ritz_values, matrix_blocks=matrix_blocks, block_lists=block_lists, inverses=inverses, panels=panels, separator_map=separator_map, separator_shift=separator_shift)


HIGHEST = lax.Precision.HIGHEST

def reference(search_vectors, ritz_values, matrix_blocks, block_lists, inverses, panels, separator_map, separator_shift):
    by_block = search_vectors.reshape(BLOCKS, BLK, VECS)

    def local_rows(operands):
        matrices, listed = operands
        return jnp.einsum('bkij,bkjm->bim', matrices, by_block[listed], precision=HIGHEST)
    product = lax.map(local_rows, (matrix_blocks.reshape(SUBS, NBLK, DEGREE, BLK, BLK), block_lists.reshape(SUBS, NBLK, DEGREE)))
    residual = product.reshape(NROWS, VECS) - search_vectors * ritz_values[None, :]
    res_blocks = residual.reshape(BLOCKS, BLK, VECS)
    one_hot = (separator_map[:, :, None] == jnp.arange(SEP_GROUPS, dtype=jnp.int32)[None, None, :]).astype(jnp.float32)
    weighted = jnp.zeros((NROWS, VECS), jnp.float32)
    for node_number in range(NODES):
        angle = math.pi * (node_number + 0.5) / NODES
        real_shift = math.cos(angle)
        imag_shift = math.sin(angle)
        first_guess = jnp.einsum('cbij,bjm->cbim', inverses[node_number], res_blocks, precision=HIGHEST)
        first_guess = first_guess.reshape(2, SUBS, ROWS, VECS)
        partial_value = jnp.einsum('tsr,ctrm->ctsm', panels, first_guess, precision=HIGHEST).reshape(2, SUBS, SEP_BLOCKS, BLK, VECS)
        separator = jnp.einsum('tpg,ctpkm->cgkm', one_hot, partial_value, precision=HIGHEST).reshape(2, GSEP, VECS)
        real_gap = (real_shift - separator_shift)[:, None]
        modulus = real_gap * real_gap + imag_shift * imag_shift
        real_part = separator[0]
        imag_part = separator[1]
        coarse = jnp.stack([(real_part * real_gap + imag_part * imag_shift) / modulus, (imag_part * real_gap - real_part * imag_shift) / modulus]).reshape(2, SEP_GROUPS, BLK, VECS)
        picked = jnp.einsum('tpg,cgkm->ctpkm', one_hot, coarse, precision=HIGHEST).reshape(2, SUBS, SEP, VECS)
        correction = jnp.einsum('tsr,ctsm->ctrm', panels, picked, precision=HIGHEST).reshape(2, BLOCKS, BLK, VECS)
        products = jnp.einsum('cbij,dbjm->cdbim', inverses[node_number], correction, precision=HIGHEST).reshape(2, 2, NROWS, VECS)
        first_flat = first_guess.reshape(2, NROWS, VECS)
        sol_real = first_flat[0] - (products[0, 0] - products[1, 1])
        sol_imag = first_flat[1] - (products[0, 1] + products[1, 0])
        weight_real = 2.0 * real_shift / NODES
        weight_imag = 2.0 * imag_shift / NODES
        weighted = weighted + weight_real * sol_real - weight_imag * sol_imag
    update = search_vectors - weighted
    factor = lax.rsqrt(lax.optimization_barrier(jnp.mean(update * update, axis=0)) + 1e-06)
    return update * factor[None, :]
```

```python
import functools
import math

import jax
import jax.numpy as jnp
from jax import lax
from jax.experimental import pallas as pl
from jax.experimental.pallas import tpu as pltpu
from jax.sharding import PartitionSpec as P

HALO_BLOCKS = 4
PIECES = 2
VMEM = pltpu.VMEM
SMEM = pltpu.SMEM


def split(x):
    hi = x.astype(jnp.bfloat16)
    lo = (x - hi.astype(jnp.float32)).astype(jnp.bfloat16)
    return hi, lo


dot = functools.partial(jnp.dot, preferred_element_type=jnp.float32)


def dot_halves(a, b):
    (a_hi, a_lo), (b_hi, b_lo) = a, b
    return dot(a_hi, b_hi) + (dot(a_hi, b_lo) + dot(a_lo, b_hi))


def stack_left(x):
    hi, lo = split(x)
    return jnp.concatenate([hi, hi, lo], axis=1)


def stack_right(x):
    hi, lo = split(x)
    return jnp.concatenate([hi, lo, hi], axis=0)


def meet(targets):
    barrier = pltpu.get_barrier_semaphore()
    for present, target in targets:
        pl.when(present)(
            functools.partial(
                pl.semaphore_signal,
                barrier, inc=1, device_id=target, device_id_type=pl.DeviceIdType.MESH,
            )
        )
    pl.semaphore_wait(barrier, sum(jnp.where(present, 1, 0) for present, _ in targets))


def remote(src, dst, send, recv, target):
    return pltpu.make_async_remote_copy(
        src_ref=src,
        dst_ref=dst,
        send_sem=send,
        recv_sem=recv,
        device_id=target,
        device_id_type=pl.DeviceIdType.MESH,
    )


def inner_size(subs):
    return max(k for k in range(1, subs + 1) if subs % k == 0 and k * k <= subs)


def begin(copies):
    for copy in copies:
        copy.start()


def finish(copies):
    for copy in copies:
        copy.wait()


def kernel(
    subs, nodes, inner,
    index_hbm, map_hbm, ritz_hbm, shift_hbm, vectors_hbm, blocks_hbm, inverses_hbm, panel_hbm,
    out_ref, factor_ref,
    index_ref, map_ref, ritz_ref, shift_ref,
    padded, blocks, inverses, panel, shift_columns, by_real, by_imag, maps, residual, partial,
    blocks_cat, inverses_cat,
    panel_hi, panel_lo, turned_hi, turned_lo, folds, guess_hi, guess_lo,
    part, near, dense, far, coarse, picked, back, value_ref, weighted, shares, landed, sums,
    table_sem, load_sem, halo_send, halo_recv, map_send, map_recv, node_send, node_recv,
    sep_send, sep_recv, far_send, far_recv, share_send, share_recv, sum_send, sum_recv,
):
    sub, node = lax.axis_index("sub"), lax.axis_index("node")
    halves, (_, size, wide) = len(padded), padded[0].shape
    count, node_local = inverses.shape[2], inverses.shape[0]
    rows_here = count // nodes
    total_nodes = node_local * nodes
    outer = subs // inner
    sep_blocks, groups = map_ref.shape[1], shift_ref.shape[0]
    exchanges = far_send.shape[0]
    pieces = turned_hi.shape[0]
    piece_rows = size // pieces
    span = piece_rows // inner
    part_cols = out_ref.shape[2]
    per_half = wide // part_cols
    place, plane = lax.rem(sub, inner), sub // inner
    base = plane * inner
    near_places = [lax.rem(place + k, inner) for k in range(1, inner)]
    near_subs = [{"sub": base + t} for t in near_places]
    corner = lax.rem(plane, 4)
    inside = (corner == 1) | (corner == 2)
    across_pair = plane + 1 - 2 * lax.rem(plane, 2)
    partner_planes = [across_pair, plane + 3 - 2 * corner]
    for i in range(exchanges - 3):
        step = 4 * 2**i
        partner_planes.append(plane + step - 2 * step * lax.rem(plane // step, 2))
    partner_planes.append(across_pair)
    other_nodes = [lax.rem(node + k, nodes) for k in range(1, nodes)]
    other_subs = [lax.rem(sub + k, subs) for k in range(1, subs)]
    row0 = node * rows_here
    lower = node < nodes // 2
    own_at = jnp.where(lower, HALO_BLOCKS, 0)

    def fetch(h):
        return pltpu.make_async_copy(
            vectors_hbm.at[:, :, pl.ds(h * wide, wide)],
            padded[h].at[pl.ds(own_at, count)],
            load_sem.at[h],
        )

    tables = [
        pltpu.make_async_copy(source, target, table_sem.at[i])
        for i, (source, target) in enumerate(
            [
                (map_hbm, map_ref), (index_hbm, index_ref),
                (ritz_hbm, ritz_ref), (shift_hbm, shift_ref),
            ]
        )
    ]
    begin(tables)
    loads = [
        pltpu.make_async_copy(inverses_hbm, inverses, load_sem.at[halves]),
        pltpu.make_async_copy(
            blocks_hbm.at[pl.ds(row0, rows_here)], blocks, load_sem.at[halves + 1]
        ),
        pltpu.make_async_copy(panel_hbm, panel, load_sem.at[halves + 2]),
    ]
    for h in range(halves):
        fetch(h).start()
    begin(loads)
    meet(
        [(True, target) for target in near_subs]
        + [(True, {"node": o}) for o in other_nodes]
        + [(sub > 0, {"sub": lax.rem(sub + subs - 1, subs)})]
        + [(sub < subs - 1, {"sub": lax.rem(sub + 1, subs)})]
        + [
            (inside if 0 < i < exchanges - 1 else True, {"sub": partner * inner + place})
            for i, partner in enumerate(partner_planes[:-1])
        ]
    )

    halo_target = {"sub": lax.rem(sub + subs + jnp.where(lower, 1, -1), subs)}
    sends_halo = jnp.where(lower, sub < subs - 1, sub > 0)
    takes_halo = jnp.where(lower, sub > 0, sub < subs - 1)

    def halo(h):
        return remote(
            padded[h].at[pl.ds(jnp.where(lower, count, 0), HALO_BLOCKS)],
            padded[h].at[pl.ds(jnp.where(lower, 0, count), HALO_BLOCKS)],
            halo_send.at[h], halo_recv.at[h], halo_target,
        )

    def send_halo(h):
        @pl.when(sends_halo)
        def _():
            halo(h).start()

    for h in range(halves):
        fetch(h).wait()
    send_halo(0)
    finish(tables)
    for p in range(sep_blocks):
        value = map_ref[0, p].astype(jnp.float32)
        maps[0, p] = jnp.full(maps.shape[2:], value, jnp.float32)
    tell = [
        remote(maps.at[0], maps.at[inner - 1 - k], map_send, map_recv, t)
        for k, t in enumerate(near_subs)
    ]
    begin(tell)

    def constant(values):
        chosen = jnp.float32(values[0])
        for k in range(1, nodes):
            chosen = jnp.where(node == k, jnp.float32(values[k]), chosen)
        return chosen

    angles = [
        [math.pi * (k * node_local + n + 0.5) / total_nodes for k in range(nodes)]
        for n in range(node_local)
    ]
    real_shift = [constant([math.cos(a) for a in row]) for row in angles]
    imag_shift = [constant([math.sin(a) for a in row]) for row in angles]
    real_weight = [constant([2.0 * math.cos(a) / total_nodes for a in row]) for row in angles]
    imag_weight = [constant([2.0 * math.sin(a) / total_nodes for a in row]) for row in angles]

    loads[0].wait()

    def prepare(b, carry):
        for n in range(node_local):
            real, imag = inverses[n, 0, b], inverses[n, 1, b]
            top = 2 * n * size
            inverses_cat[b, top : top + size] = stack_left(real)
            inverses_cat[b, top + size : top + 2 * size] = stack_left(imag)
            hi, lo = split(real_weight[n] * real - imag_weight[n] * imag)
            folds[n, b, :size, :size], folds[n, b, size:, :size] = hi, lo
            hi, lo = split(real_weight[n] * imag + imag_weight[n] * real)
            folds[n, b, :size, size:], folds[n, b, size:, size:] = hi, lo
        return carry

    lax.fori_loop(0, count, prepare, 0)
    loads[1].wait()

    def diagonal(i, carry):
        left = stack_left(blocks[i, 0])
        for h in range(halves):
            vectors = padded[h][own_at + row0 + i]
            ritz = ritz_ref[:, h * wide : (h + 1) * wide]
            partial[h, i] = dot(left, stack_right(vectors)) - vectors * ritz
        for q in range(1, blocks.shape[1]):
            blocks_cat[i, :, 3 * size * (q - 1) : 3 * size * q] = stack_left(blocks[i, q])
        return carry

    lax.fori_loop(0, rows_here, diagonal, 0)
    loads[2].wait()
    for p in range(sep_blocks):
        hi, lo = split(panel[p * size : (p + 1) * size])
        panel_hi[p * size : (p + 1) * size] = hi
        panel_lo[p * size : (p + 1) * size] = lo

    for g in range(groups):
        shift_columns[...] = jnp.broadcast_to(shift_ref[g : g + 1, :], (size, size)).T
        for r in range(pieces):
            columns = shift_columns[pl.ds(pl.multiple_of(r * piece_rows + place * span, 8), span), :]
            for n in range(node_local):
                gap = real_shift[n] - columns
                modulus = gap * gap + imag_shift[n] * imag_shift[n]
                by_real[n, r, g] = gap / modulus
                by_imag[n, r, g] = imag_shift[n] / modulus

    def turn(r, p):
        hi, lo = split(
            jnp.concatenate(
                [
                    panel[q * size + r * piece_rows : q * size + (r + 1) * piece_rows]
                    for q in range(p * pieces, (p + 1) * pieces)
                ],
                axis=0,
            ).T
        )
        turned_hi[r, :, p * size : (p + 1) * size] = hi
        turned_lo[r, :, p * size : (p + 1) * size] = lo

    def node_copies(h, i):
        return [
            remote(
                residual.at[h, row0 + i], residual.at[h, row0 + i],
                node_send, node_recv.at[k, h, i], {"node": o},
            )
            for k, o in enumerate(other_nodes)
        ]

    def residual_half(h):
        @pl.when(takes_halo)
        def _():
            halo(h).wait_recv()

        @pl.when(sends_halo)
        def _():
            halo(h).wait_send()

        if h < halves - 1:
            send_halo(h + 1)

        def step(i, carry):
            rights = []
            for q in range(1, blocks.shape[1]):
                spot = index_ref[q, row0 + i] - sub * count + own_at
                spot = jnp.clip(spot, 0, padded[h].shape[0] - 1)
                rights.append(stack_right(padded[h][spot]))
            total = partial[h, i] + dot(blocks_cat[i], jnp.concatenate(rights, axis=0))
            residual[h, row0 + i] = total
            begin(node_copies(h, i))
            return carry

        lax.fori_loop(0, rows_here, step, 0)

    def guess_half(h):
        def one(b):
            value = dot(inverses_cat[b], stack_right(residual[h, b]))
            hi, lo = split(value)
            for n in range(node_local):
                for c in range(2):
                    rows = slice((2 * n + c) * size, (2 * n + c + 1) * size)
                    k = h * node_local + n
                    guess_hi[k, b, :, c * wide : (c + 1) * wide] = hi[rows]
                    guess_lo[k, b, :, c * wide : (c + 1) * wide] = lo[rows]

        def mine(i, carry):
            one(row0 + i)
            return carry

        lax.fori_loop(0, rows_here, mine, 0)

        def theirs(i, carry):
            for copy in node_copies(h, i):
                copy.wait_recv()
            for k in range(nodes - 1):
                one(lax.rem(node + nodes - 1 - k, nodes) * rows_here + i)
            return carry

        lax.fori_loop(0, rows_here, theirs, 0)

    def rows_of(r, t):
        return pl.ds(pl.multiple_of(r * piece_rows + t * span, 8), span)

    def there_near(j):
        k, r = divmod(j, pieces)
        return [
            remote(
                part.at[k, :, :, rows_of(r, t), :], near.at[j, inner - 2 - i],
                sep_send.at[0], sep_recv.at[j, 0], near_subs[i],
            )
            for i, t in enumerate(near_places)
        ]

    def across(j, i):
        if i == 0:
            source, target = dense.at[j], far.at[j, 0]
        elif i < exchanges - 1:
            source, target = far.at[j, i - 1], far.at[j, i]
        else:
            source, target = coarse.at[j], coarse.at[j]
        return remote(
            source, target, far_send.at[i], far_recv.at[j, i % (exchanges - 1)],
            {"sub": partner_planes[i] * inner + place},
        )

    def home_near(j):
        return [
            remote(
                picked.at[j, i],
                back.at[j, :, :, pl.ds(pl.multiple_of(place * span, 8), span), :],
                sep_send.at[1], sep_recv.at[j, 1], near_subs[i],
            )
            for i in range(inner - 1)
        ]

    def stage_a(k):
        rights = (
            guess_hi[k].reshape(count * size, 2 * wide),
            guess_lo[k].reshape(count * size, 2 * wide),
        )
        value = dot_halves((panel_hi[...], panel_lo[...]), rights)
        value = value.reshape(sep_blocks, size, 2 * wide)
        part[k, 0] = value[:, :, :wide]
        part[k, 1] = value[:, :, wide:]
        for r in range(pieces):
            begin(there_near(k * pieces + r))

    def stage_b(j):
        k, r = divmod(j, pieces)
        remote(near.at[j], near.at[j], sep_send.at[0], sep_recv.at[j, 0], near_subs[0]).wait_recv()
        own = rows_of(r, place)
        for c in range(2):
            totals = [jnp.zeros((span, wide), jnp.float32) for _ in range(groups)]
            for t in range(inner):
                for p in range(sep_blocks):
                    value = part[k, c, p, own, :] if t == 0 else near[j, t - 1, c, p]
                    here = jnp.broadcast_to(maps[t, p, 0:1], (span, wide))
                    for g in range(groups):
                        totals[g] = totals[g] + jnp.where(here == float(g), value, 0.0)
            for g in range(groups):
                dense[j, c, g] = totals[g]

        @pl.when(jnp.logical_not(inside))
        def _():
            across(j, 0).start()


    def stage_c(j, i):
        k, r = divmod(j, pieces)
        n = k % node_local

        @pl.when(inside)
        def _():
            across(j, i).wait_recv()
            value = far[j, i] + (far[j, i - 1] if i > 0 else dense[j])
            if i < exchanges - 2:
                far[j, i] = value
            else:
                for g in range(groups):
                    scale_real, scale_imag = by_real[n, r, g], by_imag[n, r, g]
                    real, imag = value[0, g], value[1, g]
                    coarse[j, 0, g] = real * scale_real + imag * scale_imag
                    coarse[j, 1, g] = imag * scale_real - real * scale_imag
            across(j, i + 1).start()

    def stage_d(j):
        @pl.when(jnp.logical_not(inside))
        def _():
            across(j, exchanges - 1).wait_recv()

        copies = home_near(j)
        for t in [*range(1, inner), 0]:
            for p in range(sep_blocks):
                here = jnp.broadcast_to(maps[t, p, 0:1], (span, wide))
                for c in range(2):
                    value = coarse[j, c, 0]
                    for g in range(1, groups):
                        value = jnp.where(here == float(g), coarse[j, c, g], value)
                    if t == 0:
                        own = pl.ds(pl.multiple_of(place * span, 8), span)
                        back[j, c, p, own, :] = value
                    else:
                        picked[j, t - 1, c, p] = value
            if t > 0:
                copies[t - 1].start()

    def share_copies(o, k, b):
        return remote(
            shares.at[o, b], landed.at[k, b], share_send, share_recv.at[k, b], {"node": o}
        )

    def stage_e(j):
        k, r = divmod(j, pieces)
        h, n = divmod(k, node_local)
        come = picked.at[j]
        remote(come, come, sep_send.at[1], sep_recv.at[j, 1], near_subs[0]).wait_recv()
        right = jnp.concatenate(
            [back[j, c].reshape(sep_blocks * piece_rows, wide) for c in range(2)], axis=1
        )
        value = dot_halves((turned_hi[r], turned_lo[r]), split(right))
        value = value.reshape(count, size, 2 * wide)
        if r > 0:
            value = value + value_ref[...]
        if r < pieces - 1:
            value_ref[...] = value
            return
        for b in range(count):
            below = jnp.concatenate(
                [residual[h, b] - value[b, :, :wide], value[b, :, wide:]], axis=0
            )
            new = dot(folds[n, b], jnp.concatenate(split(below), axis=1))
            new = new[:size, :wide] + (new[:size, wide:] + new[size:, :wide])
            if n > 0:
                new = new + weighted[h, b]
            if n < node_local - 1:
                weighted[h, b] = new
                continue
            for m in range(per_half):
                shares[h * per_half + m, b] = new[:, m * part_cols : (m + 1) * part_cols]
            for s, o in enumerate(other_nodes):

                @pl.when(o // per_half == h)
                def _():
                    share_copies(o, s, b).start()

    for r in range(pieces):
        for p in range(sep_blocks // pieces):
            turn(r, p)
    events = []
    for h in range(halves):
        first = 6.5 * h
        events += [(first - 4.7, residual_half, (h,)), (first - 3.7, guess_half, (h,))]
        for n in range(node_local):
            events.append((first - 1.8 + 1.8 * n, stage_a, (h * node_local + n,)))
    others_maps = maps.at[pl.ds(1, inner - 1)]
    told = remote(others_maps, others_maps, map_send, map_recv, near_subs[0])
    events.append((3.9, finish, ([told],)))
    total_pieces = node_local * halves * pieces
    wire, hop = 2.7, 5.0
    for j in range(total_pieces):
        come = 4.0 + wire * j
        events.append((come, stage_b, (j,)))
        for i in range(exchanges - 1):
            come += hop
            events.append((come, stage_c, (j, i)))
        come += hop
        events.append((come, stage_d, (j,)))
        come = max(come, 1.0 + wire * (total_pieces + j)) + wire + 1.5
        events.append((come, stage_e, (j,)))
    for _, stage, which in sorted(events, key=lambda event: event[0]):
        stage(*which)

    def own_vectors(b):
        vectors = padded[0][own_at + b]
        for h in range(1, halves):
            vectors = jnp.where(node // per_half == h, padded[h][own_at + b], vectors)
        chosen = vectors[:, :part_cols]
        for m in range(1, per_half):
            columns = vectors[:, m * part_cols : (m + 1) * part_cols]
            chosen = jnp.where(lax.rem(node, per_half) == m, columns, chosen)
        return chosen

    def update_step(b, squares):
        total = own_vectors(b) - shares[node, b]
        for k, o in enumerate(other_nodes):
            share_copies(o, k, b).wait_recv()
            total = total - landed[k, b]
        out_ref[b] = total
        return squares + jnp.sum(total * total, axis=0, keepdims=True)

    squares = lax.fori_loop(0, count, update_step, jnp.zeros((1, part_cols), jnp.float32))
    sums[sub] = jnp.broadcast_to(squares, (8, part_cols))
    spread = [
        remote(sums.at[sub], sums.at[sub], sum_send, sum_recv, {"sub": o})
        for o in other_subs
    ]
    begin(spread)

    def left(whole, sem):
        remote(whole, whole, sem, sum_recv, near_subs[0]).wait_send()

    left(residual.at[:, pl.ds(0, (nodes - 1) * rows_here)], node_send)
    left(near, sep_send.at[0])
    left(picked, sep_send.at[1])
    left(landed, share_send)

    @pl.when(inside)
    def _():
        for i in range(1, exchanges):
            left(coarse, far_send.at[i])

    @pl.when(jnp.logical_not(inside))
    def _():
        left(coarse, far_send.at[0])

    others_sums = sums.at[pl.ds(0, subs - 1)]
    remote(others_sums, others_sums, sum_send, sum_recv, near_subs[0]).wait()
    total = sums[0]
    for t in range(1, subs):
        total = total + sums[t]
    rows = count * size * subs
    factor_ref[...] = lax.rsqrt(total[0:1] / rows + 1e-06)


def shards(
    search_vectors,
    ritz_values,
    matrix_blocks,
    block_lists,
    inverses,
    panels,
    separator_map,
    separator_shift,
):
    row_count, width = search_vectors.shape
    count, degree, size, _ = matrix_blocks.shape
    nodes, subs = lax.axis_size("node"), lax.axis_size("sub")
    node_local = inverses.shape[0]
    col_count = width // nodes
    vectors = search_vectors.reshape(count, size, width)

    inner = inner_size(subs)
    outer = subs // inner
    sep_blocks = separator_map.shape[1]
    groups = separator_shift.shape[0] // size
    wide = size
    halves = width // wide
    rows_here = count // nodes
    pieces = PIECES
    span = size // pieces // inner
    chunks = node_local * halves
    parts = chunks * pieces
    panel_rows, panel_cols = panels.shape[1:]
    exchanges = 3 + (outer // 4 - 1).bit_length()
    assert outer == 4 * 2 ** (exchanges - 3)
    assert nodes % 2 == 0 and count % nodes == 0 and 2 * HALO_BLOCKS <= count
    assert nodes % halves == 0 and span % 8 == 0 and sep_blocks % pieces == 0
    f32, bf16 = jnp.float32, jnp.bfloat16
    dma = pltpu.SemaphoreType.DMA
    updated, factor = pl.pallas_call(
        functools.partial(kernel, subs, nodes, inner),
        out_shape=[
            jax.ShapeDtypeStruct((count, size, col_count), f32),
            jax.ShapeDtypeStruct((1, col_count), f32),
        ],
        in_specs=[pl.BlockSpec(memory_space=pltpu.HBM)] * 4
        + [pl.BlockSpec(memory_space=pl.ANY)] * 4,
        out_specs=[pl.BlockSpec(memory_space=VMEM)] * 2,
        scratch_shapes=[
            SMEM((degree, count), jnp.int32),
            SMEM(separator_map.shape, jnp.int32),
            VMEM((1, width), f32),
            VMEM((groups, size), f32),
            [VMEM((count + HALO_BLOCKS, size, wide), f32)] * halves,
            VMEM((rows_here, degree, size, size), f32),
            VMEM(inverses.shape, f32),
            VMEM((panel_rows, panel_cols), f32),
            VMEM((size, size), f32),
            VMEM((node_local, pieces, groups, span, wide), f32),
            VMEM((node_local, pieces, groups, span, wide), f32),
            VMEM((inner, sep_blocks, 8, wide), f32),
            VMEM((halves, count, size, wide), f32),
            VMEM((halves, rows_here, size, wide), f32),
            VMEM((rows_here, size, 3 * (degree - 1) * size), bf16),
            VMEM((count, 2 * node_local * size, 3 * size), bf16),
            VMEM((panel_rows, panel_cols), bf16),
            VMEM((panel_rows, panel_cols), bf16),
            VMEM((pieces, panel_cols, panel_rows // pieces), bf16),
            VMEM((pieces, panel_cols, panel_rows // pieces), bf16),
            VMEM((node_local, count, 2 * size, 2 * size), bf16),
            VMEM((chunks, count, size, 2 * wide), bf16),
            VMEM((chunks, count, size, 2 * wide), bf16),
            VMEM((chunks, 2, sep_blocks, size, wide), f32),
            VMEM((parts, inner - 1, 2, sep_blocks, span, wide), f32),
            VMEM((parts, 2, groups, span, wide), f32),
            VMEM((parts, exchanges - 1, 2, groups, span, wide), f32),
            VMEM((parts, 2, groups, span, wide), f32),
            VMEM((parts, inner - 1, 2, sep_blocks, span, wide), f32),
            VMEM((parts, 2, sep_blocks, size // pieces, wide), f32),
            VMEM((count, size, 2 * wide), f32),
            VMEM((halves, count, size, wide), f32),
            VMEM((nodes, count, size, col_count), f32),
            VMEM((nodes - 1, count, size, col_count), f32),
            VMEM((subs, 8, col_count), f32),
            dma((4,)),
            dma((halves + 3,)),
            dma((halves,)),
            dma((halves,)),
            dma,
            dma,
            dma,
            dma((nodes - 1, halves, rows_here)),
            dma((2,)),
            dma((parts, 2)),
            dma((exchanges,)),
            dma((parts, exchanges - 1)),
            dma,
            dma((nodes - 1, count)),
            dma,
            dma,
        ],
        compiler_params=pltpu.CompilerParams(
            collective_id=0, has_side_effects=True, vmem_limit_bytes=54400 * 1024
        ),
        name="update",
    )(
        *(
            pltpu.with_memory_space_constraint(x, pltpu.HBM)
            for x in (
                block_lists.T, separator_map, ritz_values[None],
                separator_shift.reshape(groups, size),
            )
        ),
        vectors, matrix_blocks, inverses, panels[0],
    )
    return (updated * factor[None]).reshape(row_count, col_count)


def solution(mesh):
    return jax.shard_map(
        shards,
        mesh=mesh,
        in_specs=(
            P("sub", None),
            P(),
            P("sub", None, None, None),
            P("sub", None),
            P("node", None, "sub", None, None),
            P("sub", None, None),
            P("sub", None),
            P(),
        ),
        out_specs=P("sub", "node"),
        check_vma=False,
    )
```

```python
import functools
import math

import jax
import jax.numpy as jnp
from jax import lax
from jax.experimental import pallas as pl
from jax.experimental.pallas import tpu as pltpu
from jax.sharding import PartitionSpec as P

HALO_BLOCKS = 4
PIECES = 2
SHARES = 2
VMEM = pltpu.VMEM
SMEM = pltpu.SMEM


def split(x):
    hi = x.astype(jnp.bfloat16)
    lo = (x - hi.astype(jnp.float32)).astype(jnp.bfloat16)
    return hi, lo


dot = functools.partial(jnp.dot, preferred_element_type=jnp.float32)


def dot_halves(a, b):
    (a_hi, a_lo), (b_hi, b_lo) = a, b
    return dot(a_hi, b_hi) + (dot(a_hi, b_lo) + dot(a_lo, b_hi))


def stack_left(x):
    hi, lo = split(x)
    return jnp.concatenate([hi, hi, lo], axis=1)


def stack_right(x):
    hi, lo = split(x)
    return jnp.concatenate([hi, lo, hi], axis=0)


def meet(targets):
    barrier = pltpu.get_barrier_semaphore()
    for present, target in targets:
        pl.when(present)(
            functools.partial(
                pl.semaphore_signal,
                barrier, inc=1, device_id=target, device_id_type=pl.DeviceIdType.MESH,
            )
        )
    pl.semaphore_wait(barrier, sum(jnp.where(present, 1, 0) for present, _ in targets))


def remote(src, dst, send, recv, target):
    return pltpu.make_async_remote_copy(
        src_ref=src,
        dst_ref=dst,
        send_sem=send,
        recv_sem=recv,
        device_id=target,
        device_id_type=pl.DeviceIdType.MESH,
    )


def inner_size(subs):
    return max(k for k in range(1, subs + 1) if subs % k == 0 and k * k <= subs)


def begin(copies):
    for copy in copies:
        copy.start()


def finish(copies):
    for copy in copies:
        copy.wait()


def kernel(
    subs, nodes, inner,
    index_hbm, map_hbm, ritz_hbm, shift_hbm, vectors_hbm, blocks_hbm, inverses_hbm, panel_hbm,
    out_ref, factor_ref,
    index_ref, map_ref, ritz_ref, shift_ref,
    padded, blocks, inverses, panel, shift_columns, by_real, by_imag, maps, residual, partial,
    blocks_cat, inverses_cat,
    panel_hi, panel_lo, turned_hi, turned_lo, folds, guess_hi, guess_lo,
    part, near, dense, far, coarse, picked, back, value_ref, weighted, shares, landed, sums,
    table_sem, load_sem, halo_send, halo_recv, map_send, map_recv, node_send, node_recv,
    sep_send, sep_recv, far_send, far_recv, share_send, share_recv, sum_send, sum_recv,
):
    sub, node = lax.axis_index("sub"), lax.axis_index("node")
    halves, (_, size, wide) = len(padded), padded[0].shape
    count, node_local = inverses.shape[2], inverses.shape[0]
    rows_here = count // nodes
    total_nodes = node_local * nodes
    outer = subs // inner
    sep_blocks, groups = map_ref.shape[1], shift_ref.shape[0]
    exchanges = far_send.shape[0]
    pieces = turned_hi.shape[0]
    piece_rows = size // pieces
    span = piece_rows // inner
    part_cols = out_ref.shape[2]
    per_half = wide // part_cols
    place, plane = lax.rem(sub, inner), sub // inner
    base = plane * inner
    near_places = [lax.rem(place + k, inner) for k in range(1, inner)]
    near_subs = [{"sub": base + t} for t in near_places]
    corner = lax.rem(plane, 4)
    inside = (corner == 1) | (corner == 2)
    across_pair = plane + 1 - 2 * lax.rem(plane, 2)
    partner_planes = [across_pair, plane + 3 - 2 * corner]
    for i in range(exchanges - 3):
        step = 4 * 2**i
        partner_planes.append(plane + step - 2 * step * lax.rem(plane // step, 2))
    partner_planes.append(across_pair)
    other_nodes = [lax.rem(node + k, nodes) for k in range(1, nodes)]
    digits = [lax.rem(sub // 2**i, 2) for i in range((subs - 1).bit_length())]
    other_subs = [
        sub + sum(2**i * (1 - 2 * d) for i, d in enumerate(digits) if k // 2**i % 2)
        for k in range(subs - 1, 0, -1)
    ]
    row0 = node * rows_here
    lower = node < nodes // 2
    own_at = jnp.where(lower, HALO_BLOCKS, 0)

    def fetch(h):
        return pltpu.make_async_copy(
            vectors_hbm.at[:, :, pl.ds(h * wide, wide)],
            padded[h].at[pl.ds(own_at, count)],
            load_sem.at[h],
        )

    tables = [
        pltpu.make_async_copy(source, target, table_sem.at[i])
        for i, (source, target) in enumerate(
            [
                (map_hbm, map_ref), (index_hbm, index_ref),
                (ritz_hbm, ritz_ref), (shift_hbm, shift_ref),
            ]
        )
    ]
    begin(tables)
    loads = [
        pltpu.make_async_copy(inverses_hbm, inverses, load_sem.at[halves]),
        pltpu.make_async_copy(
            blocks_hbm.at[pl.ds(row0, rows_here)], blocks, load_sem.at[halves + 1]
        ),
        pltpu.make_async_copy(panel_hbm, panel, load_sem.at[halves + 2]),
    ]
    for h in range(halves):
        fetch(h).start()
    begin(loads)
    meet(
        [(True, target) for target in near_subs]
        + [(True, {"node": o}) for o in other_nodes]
        + [(sub > 0, {"sub": lax.rem(sub + subs - 1, subs)})]
        + [(sub < subs - 1, {"sub": lax.rem(sub + 1, subs)})]
        + [
            (inside if 0 < i < exchanges - 1 else True, {"sub": partner * inner + place})
            for i, partner in enumerate(partner_planes[:-1])
        ]
    )

    halo_target = {"sub": lax.rem(sub + subs + jnp.where(lower, 1, -1), subs)}
    sends_halo = jnp.where(lower, sub < subs - 1, sub > 0)
    takes_halo = jnp.where(lower, sub > 0, sub < subs - 1)

    def halo(h):
        rows = pl.ds(jnp.where(lower, count - HALO_BLOCKS, 0), HALO_BLOCKS)
        return remote(
            padded[h].at[pl.ds(jnp.where(lower, count, 0), HALO_BLOCKS)],
            padded[h].at[pl.ds(jnp.where(lower, 0, count), HALO_BLOCKS)],
            halo_send.at[h], halo_recv.at[h], halo_target,
        )

    def send_halo(h):
        @pl.when(sends_halo)
        def _():
            halo(h).start()

    fetch(0).wait()
    send_halo(0)
    finish(tables)
    for p in range(sep_blocks):
        value = map_ref[0, p].astype(jnp.float32)
        maps[0, p] = jnp.full(maps.shape[2:], value, jnp.float32)
    tell = [
        remote(maps.at[0], maps.at[inner - 1 - k], map_send, map_recv, t)
        for k, t in enumerate(near_subs)
    ]
    begin(tell)

    def constant(values):
        chosen = jnp.float32(values[0])
        for k in range(1, nodes):
            chosen = jnp.where(node == k, jnp.float32(values[k]), chosen)
        return chosen

    angles = [
        [math.pi * (k * node_local + n + 0.5) / total_nodes for k in range(nodes)]
        for n in range(node_local)
    ]
    real_shift = [constant([math.cos(a) for a in row]) for row in angles]
    imag_shift = [constant([math.sin(a) for a in row]) for row in angles]
    real_weight = [constant([2.0 * math.cos(a) / total_nodes for a in row]) for row in angles]
    imag_weight = [constant([2.0 * math.sin(a) / total_nodes for a in row]) for row in angles]

    loads[0].wait()

    def prepare(b, carry):
        for n in range(node_local):
            real, imag = inverses[n, 0, b], inverses[n, 1, b]
            top = 2 * n * size
            inverses_cat[b, top : top + size] = stack_left(real)
            inverses_cat[b, top + size : top + 2 * size] = stack_left(imag)
            hi, lo = split(real_weight[n] * real - imag_weight[n] * imag)
            folds[n, b, :size, :size], folds[n, b, size:, :size] = hi, lo
            hi, lo = split(real_weight[n] * imag + imag_weight[n] * real)
            folds[n, b, :size, size:], folds[n, b, size:, size:] = hi, lo
        return carry

    lax.fori_loop(0, count, prepare, 0)
    loads[1].wait()
    for h in range(1, halves):
        fetch(h).wait()

    def diagonal(i, carry):
        left = stack_left(blocks[i, 0])
        for h in range(halves):
            vectors = padded[h][own_at + row0 + i]
            ritz = ritz_ref[:, h * wide : (h + 1) * wide]
            partial[h, i] = dot(left, stack_right(vectors)) - vectors * ritz
        for q in range(1, blocks.shape[1]):
            blocks_cat[i, :, 3 * size * (q - 1) : 3 * size * q] = stack_left(blocks[i, q])
        return carry

    lax.fori_loop(0, rows_here, diagonal, 0)
    loads[2].wait()
    for p in range(sep_blocks):
        hi, lo = split(panel[p * size : (p + 1) * size])
        panel_hi[p * size : (p + 1) * size] = hi
        panel_lo[p * size : (p + 1) * size] = lo

    for g in range(groups):
        shift_columns[...] = jnp.broadcast_to(shift_ref[g : g + 1, :], (size, size)).T
        for r in range(pieces):
            columns = shift_columns[pl.ds(pl.multiple_of(r * piece_rows + place * span, 8), span), :]
            for n in range(node_local):
                gap = real_shift[n] - columns
                modulus = gap * gap + imag_shift[n] * imag_shift[n]
                by_real[n, r, g] = gap / modulus
                by_imag[n, r, g] = imag_shift[n] / modulus

    def turn(r, p):
        hi, lo = split(
            jnp.concatenate(
                [
                    panel[q * size + r * piece_rows : q * size + (r + 1) * piece_rows]
                    for q in range(p * pieces, (p + 1) * pieces)
                ],
                axis=0,
            ).T
        )
        turned_hi[r, :, p * size : (p + 1) * size] = hi
        turned_lo[r, :, p * size : (p + 1) * size] = lo

    def node_copies(h, i):
        return [
            remote(
                residual.at[h, row0 + i], residual.at[h, row0 + i],
                node_send, node_recv.at[k, h, i], {"node": o},
            )
            for k, o in enumerate(other_nodes)
        ]

    def residual_half(h):
        @pl.when(takes_halo)
        def _():
            halo(h).wait_recv()

        if h < halves - 1:
            send_halo(h + 1)

        def step(i, carry):
            rights = []
            for q in range(1, blocks.shape[1]):
                spot = index_ref[q, row0 + i] - sub * count + own_at
                spot = jnp.clip(spot, 0, padded[h].shape[0] - 1)
                rights.append(stack_right(padded[h][spot]))
            total = partial[h, i] + dot(blocks_cat[i], jnp.concatenate(rights, axis=0))
            residual[h, row0 + i] = total
            begin(node_copies(h, i))
            return carry

        lax.fori_loop(0, rows_here, step, 0)

    def guess_half(h):
        def one(b):
            value = dot(inverses_cat[b], stack_right(residual[h, b]))
            hi, lo = split(value)
            for n in range(node_local):
                for c in range(2):
                    rows = slice((2 * n + c) * size, (2 * n + c + 1) * size)
                    k = h * node_local + n
                    guess_hi[k, b, :, c * wide : (c + 1) * wide] = hi[rows]
                    guess_lo[k, b, :, c * wide : (c + 1) * wide] = lo[rows]

        def mine(i, carry):
            one(row0 + i)
            return carry

        lax.fori_loop(0, rows_here, mine, 0)

        def theirs(i, carry):
            for copy in node_copies(h, i):
                copy.wait_recv()
            for k in range(nodes - 1):
                one(lax.rem(node + nodes - 1 - k, nodes) * rows_here + i)
            return carry

        lax.fori_loop(0, rows_here, theirs, 0)

    def rows_of(r, t):
        return pl.ds(pl.multiple_of(r * piece_rows + t * span, 8), span)

    def there_near(j):
        k, r = divmod(j, pieces)
        return [
            remote(
                part.at[k, :, :, rows_of(r, t), :], near.at[j, inner - 2 - i],
                sep_send.at[0], sep_recv.at[j, 0], near_subs[i],
            )
            for i, t in enumerate(near_places)
        ]

    def across(j, i):
        if i == 0:
            source, target = dense.at[j], far.at[j, 0]
        elif i < exchanges - 1:
            source, target = far.at[j, i - 1], far.at[j, i]
        else:
            source, target = coarse.at[j], coarse.at[j]
        return remote(
            source, target, far_send.at[i], far_recv.at[j, i % (exchanges - 1)],
            {"sub": partner_planes[i] * inner + place},
        )

    def home_near(j):
        return [
            remote(
                picked.at[j, i],
                back.at[j, :, :, pl.ds(pl.multiple_of(place * span, 8), span), :],
                sep_send.at[1], sep_recv.at[j, 1], near_subs[i],
            )
            for i in range(inner - 1)
        ]

    def stage_a(k):
        rights = (
            guess_hi[k].reshape(count * size, 2 * wide),
            guess_lo[k].reshape(count * size, 2 * wide),
        )
        value = dot_halves((panel_hi[...], panel_lo[...]), rights)
        value = value.reshape(sep_blocks, size, 2 * wide)
        part[k, 0] = value[:, :, :wide]
        part[k, 1] = value[:, :, wide:]
        for r in range(pieces):
            begin(there_near(k * pieces + r))

    def stage_b(j):
        k, r = divmod(j, pieces)
        remote(near.at[j], near.at[j], sep_send.at[0], sep_recv.at[j, 0], near_subs[0]).wait_recv()
        own = rows_of(r, place)
        for c in range(2):
            totals = [jnp.zeros((span, wide), jnp.float32) for _ in range(groups)]
            for t in range(inner):
                for p in range(sep_blocks):
                    value = part[k, c, p, own, :] if t == 0 else near[j, t - 1, c, p]
                    here = jnp.broadcast_to(maps[t, p, 0:1], (span, wide))
                    for g in range(groups):
                        totals[g] = totals[g] + jnp.where(here == float(g), value, 0.0)
            for g in range(groups):
                dense[j, c, g] = totals[g]

        @pl.when(jnp.logical_not(inside))
        def _():
            across(j, 0).start()


    def stage_c(j, i):
        k, r = divmod(j, pieces)
        n = k % node_local

        @pl.when(inside)
        def _():
            across(j, i).wait_recv()
            value = far[j, i] + (far[j, i - 1] if i > 0 else dense[j])
            if i < exchanges - 2:
                far[j, i] = value
            else:
                for g in range(groups):
                    scale_real, scale_imag = by_real[n, r, g], by_imag[n, r, g]
                    real, imag = value[0, g], value[1, g]
                    coarse[j, 0, g] = real * scale_real + imag * scale_imag
                    coarse[j, 1, g] = imag * scale_real - real * scale_imag
            across(j, i + 1).start()

    def stage_d(j):
        @pl.when(jnp.logical_not(inside))
        def _():
            across(j, exchanges - 1).wait_recv()

        copies = home_near(j)
        for t in [*range(1, inner), 0]:
            for p in range(sep_blocks):
                here = jnp.broadcast_to(maps[t, p, 0:1], (span, wide))
                for c in range(2):
                    value = coarse[j, c, 0]
                    for g in range(1, groups):
                        value = jnp.where(here == float(g), coarse[j, c, g], value)
                    if t == 0:
                        own = pl.ds(pl.multiple_of(place * span, 8), span)
                        back[j, c, p, own, :] = value
                    else:
                        picked[j, t - 1, c, p] = value
            if t > 0:
                copies[t - 1].start()

    share_rows = count // SHARES

    def share_copies(o, k, part):
        rows = pl.ds(part * share_rows, share_rows)
        return remote(
            shares.at[o, rows], landed.at[k, rows], share_send, share_recv.at[k, part], {"node": o}
        )

    def stage_e(j):
        k, r = divmod(j, pieces)
        h, n = divmod(k, node_local)
        come = picked.at[j]
        remote(come, come, sep_send.at[1], sep_recv.at[j, 1], near_subs[0]).wait_recv()
        right = jnp.concatenate(
            [back[j, c].reshape(sep_blocks * piece_rows, wide) for c in range(2)], axis=1
        )
        value = dot_halves((turned_hi[r], turned_lo[r]), split(right))
        value = value.reshape(count, size, 2 * wide)
        if r > 0:
            value = value + value_ref[...]
        if r < pieces - 1:
            value_ref[...] = value
            return
        for part in range(SHARES):
            for b in range(part * share_rows, (part + 1) * share_rows):
                below = jnp.concatenate(
                    [residual[h, b] - value[b, :, :wide], value[b, :, wide:]], axis=0
                )
                new = dot(folds[n, b], jnp.concatenate(split(below), axis=1))
                new = new[:size, :wide] + (new[:size, wide:] + new[size:, :wide])
                if n > 0:
                    new = new + weighted[h, b]
                if n < node_local - 1:
                    weighted[h, b] = new
                    continue
                for m in range(per_half):
                    columns = new[:, m * part_cols : (m + 1) * part_cols]
                    shares[h * per_half + m, b] = columns
            if n < node_local - 1:
                continue
            for s, o in enumerate(other_nodes):

                @pl.when(o // per_half == h)
                def _():
                    share_copies(o, s, part).start()

    for r in range(pieces):
        for p in range(sep_blocks // pieces):
            turn(r, p)
    def left(whole, sem):
        remote(whole, whole, sem, sum_recv, near_subs[0]).wait_send()

    def all_left():
        @pl.when(sends_halo)
        def _():
            for h in range(halves):
                halo(h).wait_send()

        left(residual.at[:, pl.ds(0, (nodes - 1) * rows_here)], node_send)
        left(near, sep_send.at[0])

        @pl.when(inside)
        def _():
            for i in range(1, exchanges):
                left(coarse, far_send.at[i])

        @pl.when(jnp.logical_not(inside))
        def _():
            left(coarse, far_send.at[0])

    events = []
    for h in range(halves):
        first = 6.5 * h
        events += [(first - 4.7, residual_half, (h,)), (first - 3.7, guess_half, (h,))]
        for n in range(node_local):
            events.append((first - 1.8 + 1.8 * n, stage_a, (h * node_local + n,)))
    others_maps = maps.at[pl.ds(1, inner - 1)]
    told = remote(others_maps, others_maps, map_send, map_recv, near_subs[0])
    events.append((3.9, finish, ([told],)))
    total_pieces = node_local * halves * pieces
    wire, hop = 2.7, 5.0
    for j in range(total_pieces):
        come = 4.0 + wire * j
        events.append((come, stage_b, (j,)))
        for i in range(exchanges - 1):
            come += hop
            events.append((come, stage_c, (j, i)))
        come += hop
        events.append((come, stage_d, (j,)))
        come = max(come, 1.0 + wire * (total_pieces + j)) + wire + 1.5
        events.append((come, stage_e, (j,)))
    events.append((come - 0.1, all_left, ()))
    for _, stage, which in sorted(events, key=lambda event: event[0]):
        stage(*which)

    def own_vectors(b):
        vectors = padded[0][own_at + b]
        for h in range(1, halves):
            vectors = jnp.where(node // per_half == h, padded[h][own_at + b], vectors)
        chosen = vectors[:, :part_cols]
        for m in range(1, per_half):
            columns = vectors[:, m * part_cols : (m + 1) * part_cols]
            chosen = jnp.where(lax.rem(node, per_half) == m, columns, chosen)
        return chosen

    def update_step(b, squares):
        total = own_vectors(b) - shares[node, b]
        for k in range(nodes - 1):
            total = total - landed[k, b]
        out_ref[b] = total
        return squares + jnp.sum(total * total, axis=0, keepdims=True)

    squares = jnp.zeros((1, part_cols), jnp.float32)
    for part in range(SHARES):
        for k, o in enumerate(other_nodes):
            share_copies(o, k, part).wait_recv()
        first = part * share_rows
        squares = lax.fori_loop(first, first + share_rows, update_step, squares)
    sums[sub] = jnp.broadcast_to(squares, (8, part_cols))
    spread = [
        remote(sums.at[sub], sums.at[sub], sum_send, sum_recv, {"sub": o})
        for o in other_subs
    ]
    begin(spread)

    left(picked, sep_send.at[1])
    left(landed, share_send)
    others_sums = sums.at[pl.ds(0, subs - 1)]
    remote(others_sums, others_sums, sum_send, sum_recv, near_subs[0]).wait()
    total = sums[0]
    for t in range(1, subs):
        total = total + sums[t]
    rows = count * size * subs
    factor_ref[...] = lax.rsqrt(total[0:1] / rows + 1e-06)


def shards(
    search_vectors,
    ritz_values,
    matrix_blocks,
    block_lists,
    inverses,
    panels,
    separator_map,
    separator_shift,
):
    row_count, width = search_vectors.shape
    count, degree, size, _ = matrix_blocks.shape
    nodes, subs = lax.axis_size("node"), lax.axis_size("sub")
    node_local = inverses.shape[0]
    col_count = width // nodes
    vectors = search_vectors.reshape(count, size, width)

    inner = inner_size(subs)
    outer = subs // inner
    sep_blocks = separator_map.shape[1]
    groups = separator_shift.shape[0] // size
    wide = size
    halves = width // wide
    rows_here = count // nodes
    pieces = PIECES
    span = size // pieces // inner
    chunks = node_local * halves
    parts = chunks * pieces
    panel_rows, panel_cols = panels.shape[1:]
    exchanges = 3 + (outer // 4 - 1).bit_length()
    assert subs & (subs - 1) == 0 and count % SHARES == 0
    assert outer == 4 * 2 ** (exchanges - 3)
    assert nodes % 2 == 0 and count % nodes == 0 and 2 * HALO_BLOCKS <= count
    assert nodes % halves == 0 and span % 8 == 0 and sep_blocks % pieces == 0
    f32, bf16 = jnp.float32, jnp.bfloat16
    dma = pltpu.SemaphoreType.DMA
    updated, factor = pl.pallas_call(
        functools.partial(kernel, subs, nodes, inner),
        out_shape=[
            jax.ShapeDtypeStruct((count, size, col_count), f32),
            jax.ShapeDtypeStruct((1, col_count), f32),
        ],
        in_specs=[pl.BlockSpec(memory_space=pltpu.HBM)] * 4
        + [pl.BlockSpec(memory_space=pl.ANY)] * 4,
        out_specs=[pl.BlockSpec(memory_space=VMEM)] * 2,
        scratch_shapes=[
            SMEM((degree, count), jnp.int32),
            SMEM(separator_map.shape, jnp.int32),
            VMEM((1, width), f32),
            VMEM((groups, size), f32),
            [VMEM((count + HALO_BLOCKS, size, wide), f32)] * halves,
            VMEM((rows_here, degree, size, size), f32),
            VMEM(inverses.shape, f32),
            VMEM((panel_rows, panel_cols), f32),
            VMEM((size, size), f32),
            VMEM((node_local, pieces, groups, span, wide), f32),
            VMEM((node_local, pieces, groups, span, wide), f32),
            VMEM((inner, sep_blocks, 8, wide), f32),
            VMEM((halves, count, size, wide), f32),
            VMEM((halves, rows_here, size, wide), f32),
            VMEM((rows_here, size, 3 * (degree - 1) * size), bf16),
            VMEM((count, 2 * node_local * size, 3 * size), bf16),
            VMEM((panel_rows, panel_cols), bf16),
            VMEM((panel_rows, panel_cols), bf16),
            VMEM((pieces, panel_cols, panel_rows // pieces), bf16),
            VMEM((pieces, panel_cols, panel_rows // pieces), bf16),
            VMEM((node_local, count, 2 * size, 2 * size), bf16),
            VMEM((chunks, count, size, 2 * wide), bf16),
            VMEM((chunks, count, size, 2 * wide), bf16),
            VMEM((chunks, 2, sep_blocks, size, wide), f32),
            VMEM((parts, inner - 1, 2, sep_blocks, span, wide), f32),
            VMEM((parts, 2, groups, span, wide), f32),
            VMEM((parts, exchanges - 1, 2, groups, span, wide), f32),
            VMEM((parts, 2, groups, span, wide), f32),
            VMEM((parts, inner - 1, 2, sep_blocks, span, wide), f32),
            VMEM((parts, 2, sep_blocks, size // pieces, wide), f32),
            VMEM((count, size, 2 * wide), f32),
            VMEM((halves, count, size, wide), f32),
            VMEM((nodes, count, size, col_count), f32),
            VMEM((nodes - 1, count, size, col_count), f32),
            VMEM((subs, 8, col_count), f32),
            dma((4,)),
            dma((halves + 3,)),
            dma((halves,)),
            dma((halves,)),
            dma,
            dma,
            dma,
            dma((nodes - 1, halves, rows_here)),
            dma((2,)),
            dma((parts, 2)),
            dma((exchanges,)),
            dma((parts, exchanges - 1)),
            dma,
            dma((nodes - 1, SHARES)),
            dma,
            dma,
        ],
        compiler_params=pltpu.CompilerParams(
            collective_id=0, has_side_effects=True, vmem_limit_bytes=54400 * 1024
        ),
        name="update",
    )(
        *(
            pltpu.with_memory_space_constraint(x, pltpu.HBM)
            for x in (
                block_lists.T, separator_map, ritz_values[None],
                separator_shift.reshape(groups, size),
            )
        ),
        vectors, matrix_blocks, inverses, panels[0],
    )
    return (updated * factor[None]).reshape(row_count, col_count)


def solution(mesh):
    return jax.shard_map(
        shards,
        mesh=mesh,
        in_specs=(
            P("sub", None),
            P(),
            P("sub", None, None, None),
            P("sub", None),
            P("node", None, "sub", None, None),
            P("sub", None, None),
            P("sub", None),
            P(),
        ),
        out_specs=P("sub", "node"),
        check_vma=False,
    )
```

```python
import functools
import math

import jax
import jax.numpy as jnp
from jax import lax
from jax.experimental import pallas as pl
from jax.experimental.pallas import tpu as pltpu
from jax.sharding import PartitionSpec as P

HALO_BLOCKS = 4
PIECES = 2
SHARES = 2
VMEM = pltpu.VMEM
SMEM = pltpu.SMEM


def split(x):
    hi = x.astype(jnp.bfloat16)
    lo = (x - hi.astype(jnp.float32)).astype(jnp.bfloat16)
    return hi, lo


dot = functools.partial(jnp.dot, preferred_element_type=jnp.float32)


def dot_halves(a, b):
    (a_hi, a_lo), (b_hi, b_lo) = a, b
    return dot(a_hi, b_hi) + (dot(a_hi, b_lo) + dot(a_lo, b_hi))


def stack_left(x):
    hi, lo = split(x)
    return jnp.concatenate([hi, hi, lo], axis=1)


def stack_right(x):
    hi, lo = split(x)
    return jnp.concatenate([hi, lo, hi], axis=0)


def meet(targets):
    barrier = pltpu.get_barrier_semaphore()
    for present, target in targets:
        pl.when(present)(
            functools.partial(
                pl.semaphore_signal,
                barrier, inc=1, device_id=target, device_id_type=pl.DeviceIdType.MESH,
            )
        )
    pl.semaphore_wait(barrier, sum(jnp.where(present, 1, 0) for present, _ in targets))


def remote(src, dst, send, recv, target):
    return pltpu.make_async_remote_copy(
        src_ref=src,
        dst_ref=dst,
        send_sem=send,
        recv_sem=recv,
        device_id=target,
        device_id_type=pl.DeviceIdType.MESH,
    )


def inner_size(subs):
    return max(k for k in range(1, subs + 1) if subs % k == 0 and k * k <= subs)


def begin(copies):
    for copy in copies:
        copy.start()


def finish(copies):
    for copy in copies:
        copy.wait()


def kernel(
    subs, nodes, inner,
    index_hbm, map_hbm, ritz_hbm, shift_hbm, vectors_hbm, blocks_hbm, inverses_hbm, panel_hbm,
    out_ref, factor_ref,
    index_ref, map_ref, ritz_ref, shift_ref,
    padded, blocks, inverses, panel, shift_columns, by_real, by_imag, maps, residual, partial,
    blocks_cat, inverses_cat,
    panel_hi, panel_lo, turned_hi, turned_lo, folds, guess_hi, guess_lo,
    part, near, dense, far, coarse, picked, back, value_ref, weighted, shares, landed, sums,
    table_sem, load_sem, halo_send, halo_recv, map_send, map_recv, node_send, node_recv,
    sep_send, sep_recv, far_send, far_recv, share_send, share_recv, sum_send, sum_recv,
):
    sub, node = lax.axis_index("sub"), lax.axis_index("node")
    halves, (_, size, wide) = len(padded), padded[0].shape
    count, node_local = inverses.shape[2], inverses.shape[0]
    rows_here = count // nodes
    total_nodes = node_local * nodes
    outer = subs // inner
    sep_blocks, groups = map_ref.shape[1], shift_ref.shape[0]
    exchanges = far_send.shape[0]
    pieces = turned_hi.shape[0]
    piece_rows = size // pieces
    span = piece_rows // inner
    part_cols = out_ref.shape[2]
    per_half = wide // part_cols
    place, plane = lax.rem(sub, inner), sub // inner
    base = plane * inner

    def flipped(number, mask, width):
        digits = [i for i in range((width - 1).bit_length()) if mask // 2**i % 2]
        return number + sum(2**i * (1 - 2 * lax.rem(number // 2**i, 2)) for i in digits)

    near_places = [flipped(place, k, inner) for k in range(inner - 1, 0, -1)]
    near_subs = [{"sub": base + t} for t in near_places]
    corner = lax.rem(plane, 4)
    inside = (corner == 1) | (corner == 2)
    across_pair = plane + 1 - 2 * lax.rem(plane, 2)
    partner_planes = [across_pair, plane + 3 - 2 * corner]
    for i in range(exchanges - 3):
        step = 4 * 2**i
        partner_planes.append(plane + step - 2 * step * lax.rem(plane // step, 2))
    partner_planes.append(across_pair)
    other_nodes = [lax.rem(node + k, nodes) for k in range(1, nodes)]
    other_subs = [flipped(sub, k, subs) for k in range(subs - 1, 0, -1)]
    row0 = node * rows_here
    lower = node < nodes // 2
    own_at = jnp.where(lower, HALO_BLOCKS, 0)

    def fetch(h):
        return pltpu.make_async_copy(
            vectors_hbm.at[:, :, pl.ds(h * wide, wide)],
            padded[h].at[pl.ds(own_at, count)],
            load_sem.at[h],
        )

    tables = [
        pltpu.make_async_copy(source, target, table_sem.at[i])
        for i, (source, target) in enumerate(
            [
                (map_hbm, map_ref), (index_hbm, index_ref),
                (ritz_hbm, ritz_ref), (shift_hbm, shift_ref),
            ]
        )
    ]
    begin(tables)
    loads = [
        pltpu.make_async_copy(inverses_hbm, inverses, load_sem.at[halves]),
        pltpu.make_async_copy(
            blocks_hbm.at[pl.ds(row0, rows_here)], blocks, load_sem.at[halves + 1]
        ),
        pltpu.make_async_copy(panel_hbm, panel, load_sem.at[halves + 2]),
    ]
    for h in range(halves):
        fetch(h).start()
    begin(loads)
    meet(
        [(True, target) for target in near_subs]
        + [(True, {"node": o}) for o in other_nodes]
        + [(sub > 0, {"sub": lax.rem(sub + subs - 1, subs)})]
        + [(sub < subs - 1, {"sub": lax.rem(sub + 1, subs)})]
        + [
            (inside if 0 < i < exchanges - 1 else True, {"sub": partner * inner + place})
            for i, partner in enumerate(partner_planes[:-1])
        ]
    )

    halo_target = {"sub": lax.rem(sub + subs + jnp.where(lower, 1, -1), subs)}
    sends_halo = jnp.where(lower, sub < subs - 1, sub > 0)
    takes_halo = jnp.where(lower, sub > 0, sub < subs - 1)

    def halo(h):
        rows = pl.ds(jnp.where(lower, count - HALO_BLOCKS, 0), HALO_BLOCKS)
        return remote(
            padded[h].at[pl.ds(jnp.where(lower, count, 0), HALO_BLOCKS)],
            padded[h].at[pl.ds(jnp.where(lower, 0, count), HALO_BLOCKS)],
            halo_send.at[h], halo_recv.at[h], halo_target,
        )

    def send_halo(h):
        @pl.when(sends_halo)
        def _():
            halo(h).start()

    fetch(0).wait()
    send_halo(0)
    finish(tables)
    for p in range(sep_blocks):
        value = map_ref[0, p].astype(jnp.float32)
        maps[0, p] = jnp.full(maps.shape[2:], value, jnp.float32)
    tell = [
        remote(maps.at[0], maps.at[k + 1], map_send, map_recv, t)
        for k, t in enumerate(near_subs)
    ]
    begin(tell)

    def constant(values):
        chosen = jnp.float32(values[0])
        for k in range(1, nodes):
            chosen = jnp.where(node == k, jnp.float32(values[k]), chosen)
        return chosen

    angles = [
        [math.pi * (k * node_local + n + 0.5) / total_nodes for k in range(nodes)]
        for n in range(node_local)
    ]
    real_shift = [constant([math.cos(a) for a in row]) for row in angles]
    imag_shift = [constant([math.sin(a) for a in row]) for row in angles]
    real_weight = [constant([2.0 * math.cos(a) / total_nodes for a in row]) for row in angles]
    imag_weight = [constant([2.0 * math.sin(a) / total_nodes for a in row]) for row in angles]

    loads[0].wait()

    def prepare(b, carry):
        for n in range(node_local):
            real, imag = inverses[n, 0, b], inverses[n, 1, b]
            top = 2 * n * size
            inverses_cat[b, top : top + size] = stack_left(real)
            inverses_cat[b, top + size : top + 2 * size] = stack_left(imag)
            hi, lo = split(real_weight[n] * real - imag_weight[n] * imag)
            folds[n, b, :size, :size], folds[n, b, size:, :size] = hi, lo
            hi, lo = split(real_weight[n] * imag + imag_weight[n] * real)
            folds[n, b, :size, size:], folds[n, b, size:, size:] = hi, lo
        return carry

    lax.fori_loop(0, count, prepare, 0)
    loads[1].wait()
    for h in range(1, halves):
        fetch(h).wait()

    def diagonal(i, carry):
        left = stack_left(blocks[i, 0])
        for h in range(halves):
            vectors = padded[h][own_at + row0 + i]
            ritz = ritz_ref[:, h * wide : (h + 1) * wide]
            partial[h, i] = dot(left, stack_right(vectors)) - vectors * ritz
        for q in range(1, blocks.shape[1]):
            blocks_cat[i, :, 3 * size * (q - 1) : 3 * size * q] = stack_left(blocks[i, q])
        return carry

    lax.fori_loop(0, rows_here, diagonal, 0)
    loads[2].wait()
    for p in range(sep_blocks):
        hi, lo = split(panel[p * size : (p + 1) * size])
        panel_hi[p * size : (p + 1) * size] = hi
        panel_lo[p * size : (p + 1) * size] = lo

    for g in range(groups):
        shift_columns[...] = jnp.broadcast_to(shift_ref[g : g + 1, :], (size, size)).T
        for r in range(pieces):
            columns = shift_columns[pl.ds(pl.multiple_of(r * piece_rows + place * span, 8), span), :]
            for n in range(node_local):
                gap = real_shift[n] - columns
                modulus = gap * gap + imag_shift[n] * imag_shift[n]
                by_real[n, r, g] = gap / modulus
                by_imag[n, r, g] = imag_shift[n] / modulus

    strip = size // sep_blocks

    def turn(r, p):
        hi, lo = split(
            jnp.concatenate(
                [
                    panel[q * size + first : q * size + first + span]
                    for first in range(r * piece_rows + p * strip, r * piece_rows + (p + 1) * strip, span)
                    for q in range(sep_blocks)
                ],
                axis=0,
            ).T
        )
        turned_hi[r, :, p * size : (p + 1) * size] = hi
        turned_lo[r, :, p * size : (p + 1) * size] = lo

    def node_copies(h, i):
        return [
            remote(
                residual.at[h, row0 + i], residual.at[h, row0 + i],
                node_send, node_recv.at[k, h, i], {"node": o},
            )
            for k, o in enumerate(other_nodes)
        ]

    def residual_half(h):
        @pl.when(takes_halo)
        def _():
            halo(h).wait_recv()

        if h < halves - 1:
            send_halo(h + 1)

        def step(i, carry):
            rights = []
            for q in range(1, blocks.shape[1]):
                spot = index_ref[q, row0 + i] - sub * count + own_at
                spot = jnp.clip(spot, 0, padded[h].shape[0] - 1)
                rights.append(stack_right(padded[h][spot]))
            total = partial[h, i] + dot(blocks_cat[i], jnp.concatenate(rights, axis=0))
            residual[h, row0 + i] = total
            begin(node_copies(h, i))
            return carry

        lax.fori_loop(0, rows_here, step, 0)

    def guess_half(h):
        def one(b):
            value = dot(inverses_cat[b], stack_right(residual[h, b]))
            hi, lo = split(value)
            for n in range(node_local):
                for c in range(2):
                    rows = slice((2 * n + c) * size, (2 * n + c + 1) * size)
                    k = h * node_local + n
                    guess_hi[k, b, :, c * wide : (c + 1) * wide] = hi[rows]
                    guess_lo[k, b, :, c * wide : (c + 1) * wide] = lo[rows]

        def mine(i, carry):
            one(row0 + i)
            return carry

        lax.fori_loop(0, rows_here, mine, 0)

        def theirs(i, carry):
            for copy in node_copies(h, i):
                copy.wait_recv()
            for k in range(nodes - 1):
                one(lax.rem(node + nodes - 1 - k, nodes) * rows_here + i)
            return carry

        lax.fori_loop(0, rows_here, theirs, 0)

    def rows_of(r, t):
        return pl.ds(pl.multiple_of(r * piece_rows + t * span, 8), span)

    def there_near(j):
        k, r = divmod(j, pieces)
        return [
            remote(
                part.at[k, r, t], near.at[j, i],
                sep_send.at[0], sep_recv.at[j, 0], near_subs[i],
            )
            for i, t in enumerate(near_places)
        ]

    def across(j, i):
        if i == 0:
            source, target = dense.at[j], far.at[j, 0]
        elif i < exchanges - 1:
            source, target = far.at[j, i - 1], far.at[j, i]
        else:
            source, target = coarse.at[j], coarse.at[j]
        return remote(
            source, target, far_send.at[i], far_recv.at[j, i % (exchanges - 1)],
            {"sub": partner_planes[i] * inner + place},
        )

    def home_near(j):
        return [
            remote(
                picked.at[j, i],
                back.at[j, place],
                sep_send.at[1], sep_recv.at[j, 1], near_subs[i],
            )
            for i in range(inner - 1)
        ]

    def stage_a(k):
        rights = (
            guess_hi[k].reshape(count * size, 2 * wide),
            guess_lo[k].reshape(count * size, 2 * wide),
        )
        value = dot_halves((panel_hi[...], panel_lo[...]), rights)
        value = value.reshape(sep_blocks, size, 2 * wide)
        for r in range(pieces):
            for t in range(inner):
                first = r * piece_rows + t * span
                for c in range(2):
                    part[k, r, t, c] = value[:, first : first + span, c * wide : (c + 1) * wide]
            begin(there_near(k * pieces + r))

    def stage_b(j):
        k, r = divmod(j, pieces)
        remote(near.at[j], near.at[j], sep_send.at[0], sep_recv.at[j, 0], near_subs[0]).wait_recv()
        for c in range(2):
            totals = [jnp.zeros((span, wide), jnp.float32) for _ in range(groups)]
            for t in range(inner):
                for p in range(sep_blocks):
                    value = part[k, r, place, c, p] if t == 0 else near[j, t - 1, c, p]
                    here = jnp.broadcast_to(maps[t, p, 0:1], (span, wide))
                    for g in range(groups):
                        totals[g] = totals[g] + jnp.where(here == float(g), value, 0.0)
            for g in range(groups):
                dense[j, c, g] = totals[g]

        @pl.when(jnp.logical_not(inside))
        def _():
            across(j, 0).start()


    def stage_c(j, i):
        k, r = divmod(j, pieces)
        n = k % node_local

        @pl.when(inside)
        def _():
            across(j, i).wait_recv()
            value = far[j, i] + (far[j, i - 1] if i > 0 else dense[j])
            if i < exchanges - 2:
                far[j, i] = value
            else:
                for g in range(groups):
                    scale_real, scale_imag = by_real[n, r, g], by_imag[n, r, g]
                    real, imag = value[0, g], value[1, g]
                    coarse[j, 0, g] = real * scale_real + imag * scale_imag
                    coarse[j, 1, g] = imag * scale_real - real * scale_imag
            across(j, i + 1).start()

    def stage_d(j):
        @pl.when(jnp.logical_not(inside))
        def _():
            across(j, exchanges - 1).wait_recv()

        copies = home_near(j)
        for t in [*range(1, inner), 0]:
            for p in range(sep_blocks):
                here = jnp.broadcast_to(maps[t, p, 0:1], (span, wide))
                for c in range(2):
                    value = coarse[j, c, 0]
                    for g in range(1, groups):
                        value = jnp.where(here == float(g), coarse[j, c, g], value)
                    if t == 0:
                        back[j, place, c, p] = value
                    else:
                        picked[j, t - 1, c, p] = value
            if t > 0:
                copies[t - 1].start()

    share_rows = count // SHARES

    def share_copies(o, k, part):
        rows = pl.ds(part * share_rows, share_rows)
        return remote(
            shares.at[o, rows], landed.at[k, rows], share_send, share_recv.at[k, part], {"node": o}
        )

    def stage_e(j):
        k, r = divmod(j, pieces)
        h, n = divmod(k, node_local)
        come = picked.at[j]
        remote(come, come, sep_send.at[1], sep_recv.at[j, 1], near_subs[0]).wait_recv()
        right = jnp.concatenate(
            [back[j, :, c].reshape(sep_blocks * piece_rows, wide) for c in range(2)], axis=1
        )
        value = dot_halves((turned_hi[r], turned_lo[r]), split(right))
        value = value.reshape(count, size, 2 * wide)
        if r > 0:
            value = value + value_ref[...]
        if r < pieces - 1:
            value_ref[...] = value
            return
        for part in range(SHARES):
            for b in range(part * share_rows, (part + 1) * share_rows):
                below = jnp.concatenate(
                    [residual[h, b] - value[b, :, :wide], value[b, :, wide:]], axis=0
                )
                new = dot(folds[n, b], jnp.concatenate(split(below), axis=1))
                new = new[:size, :wide] + (new[:size, wide:] + new[size:, :wide])
                if n > 0:
                    new = new + weighted[h, b]
                if n < node_local - 1:
                    weighted[h, b] = new
                    continue
                for m in range(per_half):
                    columns = new[:, m * part_cols : (m + 1) * part_cols]
                    shares[h * per_half + m, b] = columns
            if n < node_local - 1:
                continue
            for s, o in enumerate(other_nodes):

                @pl.when(o // per_half == h)
                def _():
                    share_copies(o, s, part).start()

    for r in range(pieces):
        for p in range(sep_blocks // pieces):
            turn(r, p)
    def left(whole, sem):
        remote(whole, whole, sem, sum_recv, near_subs[0]).wait_send()

    def all_left():
        @pl.when(sends_halo)
        def _():
            for h in range(halves):
                halo(h).wait_send()

        left(residual.at[:, pl.ds(0, (nodes - 1) * rows_here)], node_send)
        left(near, sep_send.at[0])

        @pl.when(inside)
        def _():
            for i in range(1, exchanges):
                left(coarse, far_send.at[i])

        @pl.when(jnp.logical_not(inside))
        def _():
            left(coarse, far_send.at[0])

    events = []
    for h in range(halves):
        first = 6.5 * h
        events += [(first - 4.7, residual_half, (h,)), (first - 3.7, guess_half, (h,))]
        for n in range(node_local):
            events.append((first - 1.8 + 1.8 * n, stage_a, (h * node_local + n,)))
    others_maps = maps.at[pl.ds(1, inner - 1)]
    told = remote(others_maps, others_maps, map_send, map_recv, near_subs[0])
    events.append((3.9, finish, ([told],)))
    total_pieces = node_local * halves * pieces
    wire, hop = 2.7, 5.0
    for j in range(total_pieces):
        come = 4.0 + wire * j
        events.append((come, stage_b, (j,)))
        for i in range(exchanges - 1):
            come += hop
            events.append((come, stage_c, (j, i)))
        come += hop
        events.append((come, stage_d, (j,)))
        come = max(come, 1.0 + wire * (total_pieces + j)) + wire + 1.5
        events.append((come, stage_e, (j,)))
    events.append((come - 0.1, all_left, ()))
    for _, stage, which in sorted(events, key=lambda event: event[0]):
        stage(*which)

    def own_vectors(b):
        vectors = padded[0][own_at + b]
        for h in range(1, halves):
            vectors = jnp.where(node // per_half == h, padded[h][own_at + b], vectors)
        chosen = vectors[:, :part_cols]
        for m in range(1, per_half):
            columns = vectors[:, m * part_cols : (m + 1) * part_cols]
            chosen = jnp.where(lax.rem(node, per_half) == m, columns, chosen)
        return chosen

    def update_step(b, squares):
        total = own_vectors(b) - shares[node, b]
        for k in range(nodes - 1):
            total = total - landed[k, b]
        out_ref[b] = total
        return squares + jnp.sum(total * total, axis=0, keepdims=True)

    squares = jnp.zeros((1, part_cols), jnp.float32)
    for part in range(SHARES):
        for k, o in enumerate(other_nodes):
            share_copies(o, k, part).wait_recv()
        first = part * share_rows
        squares = lax.fori_loop(first, first + share_rows, update_step, squares)
    sums[sub] = jnp.broadcast_to(squares, (8, part_cols))
    spread = [
        remote(sums.at[sub], sums.at[sub], sum_send, sum_recv, {"sub": o})
        for o in other_subs
    ]
    begin(spread)

    left(picked, sep_send.at[1])
    left(landed, share_send)
    others_sums = sums.at[pl.ds(0, subs - 1)]
    remote(others_sums, others_sums, sum_send, sum_recv, near_subs[0]).wait()
    total = sums[0]
    for t in range(1, subs):
        total = total + sums[t]
    rows = count * size * subs
    factor_ref[...] = lax.rsqrt(total[0:1] / rows + 1e-06)


def shards(
    search_vectors,
    ritz_values,
    matrix_blocks,
    block_lists,
    inverses,
    panels,
    separator_map,
    separator_shift,
):
    row_count, width = search_vectors.shape
    count, degree, size, _ = matrix_blocks.shape
    nodes, subs = lax.axis_size("node"), lax.axis_size("sub")
    node_local = inverses.shape[0]
    col_count = width // nodes
    vectors = search_vectors.reshape(count, size, width)

    inner = inner_size(subs)
    outer = subs // inner
    sep_blocks = separator_map.shape[1]
    groups = separator_shift.shape[0] // size
    wide = size
    halves = width // wide
    rows_here = count // nodes
    pieces = PIECES
    span = size // pieces // inner
    chunks = node_local * halves
    parts = chunks * pieces
    panel_rows, panel_cols = panels.shape[1:]
    exchanges = 3 + (outer // 4 - 1).bit_length()
    assert subs & (subs - 1) == 0 and inner & (inner - 1) == 0 and count % SHARES == 0
    assert outer == 4 * 2 ** (exchanges - 3)
    assert nodes % 2 == 0 and count % nodes == 0 and 2 * HALO_BLOCKS <= count
    assert nodes % halves == 0 and span % 8 == 0 and size % (sep_blocks * span) == 0 and sep_blocks % pieces == 0
    f32, bf16 = jnp.float32, jnp.bfloat16
    dma = pltpu.SemaphoreType.DMA
    updated, factor = pl.pallas_call(
        functools.partial(kernel, subs, nodes, inner),
        out_shape=[
            jax.ShapeDtypeStruct((count, size, col_count), f32),
            jax.ShapeDtypeStruct((1, col_count), f32),
        ],
        in_specs=[pl.BlockSpec(memory_space=pltpu.HBM)] * 4
        + [pl.BlockSpec(memory_space=pl.ANY)] * 4,
        out_specs=[pl.BlockSpec(memory_space=VMEM)] * 2,
        scratch_shapes=[
            SMEM((degree, count), jnp.int32),
            SMEM(separator_map.shape, jnp.int32),
            VMEM((1, width), f32),
            VMEM((groups, size), f32),
            [VMEM((count + HALO_BLOCKS, size, wide), f32)] * halves,
            VMEM((rows_here, degree, size, size), f32),
            VMEM(inverses.shape, f32),
            VMEM((panel_rows, panel_cols), f32),
            VMEM((size, size), f32),
            VMEM((node_local, pieces, groups, span, wide), f32),
            VMEM((node_local, pieces, groups, span, wide), f32),
            VMEM((inner, sep_blocks, 8, wide), f32),
            VMEM((halves, count, size, wide), f32),
            VMEM((halves, rows_here, size, wide), f32),
            VMEM((rows_here, size, 3 * (degree - 1) * size), bf16),
            VMEM((count, 2 * node_local * size, 3 * size), bf16),
            VMEM((panel_rows, panel_cols), bf16),
            VMEM((panel_rows, panel_cols), bf16),
            VMEM((pieces, panel_cols, panel_rows // pieces), bf16),
            VMEM((pieces, panel_cols, panel_rows // pieces), bf16),
            VMEM((node_local, count, 2 * size, 2 * size), bf16),
            VMEM((chunks, count, size, 2 * wide), bf16),
            VMEM((chunks, count, size, 2 * wide), bf16),
            VMEM((chunks, pieces, inner, 2, sep_blocks, span, wide), f32),
            VMEM((parts, inner - 1, 2, sep_blocks, span, wide), f32),
            VMEM((parts, 2, groups, span, wide), f32),
            VMEM((parts, exchanges - 1, 2, groups, span, wide), f32),
            VMEM((parts, 2, groups, span, wide), f32),
            VMEM((parts, inner - 1, 2, sep_blocks, span, wide), f32),
            VMEM((parts, inner, 2, sep_blocks, span, wide), f32),
            VMEM((count, size, 2 * wide), f32),
            VMEM((halves, count, size, wide), f32),
            VMEM((nodes, count, size, col_count), f32),
            VMEM((nodes - 1, count, size, col_count), f32),
            VMEM((subs, 8, col_count), f32),
            dma((4,)),
            dma((halves + 3,)),
            dma((halves,)),
            dma((halves,)),
            dma,
            dma,
            dma,
            dma((nodes - 1, halves, rows_here)),
            dma((2,)),
            dma((parts, 2)),
            dma((exchanges,)),
            dma((parts, exchanges - 1)),
            dma,
            dma((nodes - 1, SHARES)),
            dma,
            dma,
        ],
        compiler_params=pltpu.CompilerParams(
            collective_id=0, has_side_effects=True, vmem_limit_bytes=54400 * 1024
        ),
        name="update",
    )(
        *(
            pltpu.with_memory_space_constraint(x, pltpu.HBM)
            for x in (
                block_lists.T, separator_map, ritz_values[None],
                separator_shift.reshape(groups, size),
            )
        ),
        vectors, matrix_blocks, inverses, panels[0],
    )
    return (updated * factor[None]).reshape(row_count, col_count)


def solution(mesh):
    return jax.shard_map(
        shards,
        mesh=mesh,
        in_specs=(
            P("sub", None),
            P(),
            P("sub", None, None, None),
            P("sub", None),
            P("node", None, "sub", None, None),
            P("sub", None, None),
            P("sub", None),
            P(),
        ),
        out_specs=P("sub", "node"),
        check_vma=False,
    )
```

```python
import functools
import math

import jax
import jax.numpy as jnp
from jax import lax
from jax.experimental import pallas as pl
from jax.experimental.pallas import tpu as pltpu
from jax.sharding import PartitionSpec as P

HALO_BLOCKS = 4
PIECES = 2
SHARES = 2
VMEM = pltpu.VMEM
SMEM = pltpu.SMEM


def split(x):
    hi = x.astype(jnp.bfloat16)
    lo = (x - hi.astype(jnp.float32)).astype(jnp.bfloat16)
    return hi, lo


dot = functools.partial(jnp.dot, preferred_element_type=jnp.float32)


def dot_halves(a, b):
    (a_hi, a_lo), (b_hi, b_lo) = a, b
    return dot(a_hi, b_hi) + (dot(a_hi, b_lo) + dot(a_lo, b_hi))


def stack_left(x):
    hi, lo = split(x)
    return jnp.concatenate([hi, hi, lo], axis=1)


def stack_right(x):
    hi, lo = split(x)
    return jnp.concatenate([hi, lo, hi], axis=0)


def meet(targets):
    barrier = pltpu.get_barrier_semaphore()
    for present, target in targets:
        pl.when(present)(
            functools.partial(
                pl.semaphore_signal,
                barrier, inc=1, device_id=target, device_id_type=pl.DeviceIdType.MESH,
            )
        )
    pl.semaphore_wait(barrier, sum(jnp.where(present, 1, 0) for present, _ in targets))


def remote(src, dst, send, recv, target):
    return pltpu.make_async_remote_copy(
        src_ref=src,
        dst_ref=dst,
        send_sem=send,
        recv_sem=recv,
        device_id=target,
        device_id_type=pl.DeviceIdType.MESH,
    )


def inner_size(subs):
    return max(k for k in range(1, subs + 1) if subs % k == 0 and k * k <= subs)


def begin(copies):
    for copy in copies:
        copy.start()


def finish(copies):
    for copy in copies:
        copy.wait()


def kernel(
    subs, nodes, inner,
    index_hbm, map_hbm, ritz_hbm, shift_hbm, vectors_hbm, blocks_hbm, inverses_hbm, panel_hbm,
    out_ref, factor_ref,
    index_ref, map_ref, ritz_ref, shift_ref,
    padded, blocks, inverses, panel, shift_columns, by_real, by_imag, maps, residual, partial,
    blocks_cat, inverses_cat,
    panel_hi, panel_lo, turned_hi, turned_lo, folds, guess_hi, guess_lo,
    part, near, dense, far, coarse, picked, back, value_ref, weighted, shares, landed, sums,
    table_sem, load_sem, halo_send, halo_recv, map_send, map_recv, node_send, node_recv,
    sep_send, sep_recv, far_send, far_recv, share_send, share_recv, sum_send, sum_recv,
):
    sub, node = lax.axis_index("sub"), lax.axis_index("node")
    halves, (_, size, wide) = len(padded), padded[0].shape
    count, node_local = inverses.shape[2], inverses.shape[0]
    rows_here = count // nodes
    total_nodes = node_local * nodes
    outer = subs // inner
    sep_blocks, groups = map_ref.shape[1], shift_ref.shape[0]
    exchanges = far_send.shape[0]
    pieces = turned_hi.shape[0]
    piece_rows = size // pieces
    span = piece_rows // inner
    part_cols = out_ref.shape[2]
    per_half = wide // part_cols
    place, plane = lax.rem(sub, inner), sub // inner
    base = plane * inner

    def flipped(number, mask, width):
        digits = [i for i in range((width - 1).bit_length()) if mask // 2**i % 2]
        return number + sum(2**i * (1 - 2 * lax.rem(number // 2**i, 2)) for i in digits)

    near_places = [flipped(place, k, inner) for k in range(inner - 1, 0, -1)]
    near_subs = [{"sub": base + t} for t in near_places]
    corner = lax.rem(plane, 4)
    inside = (corner == 1) | (corner == 2)
    across_pair = plane + 1 - 2 * lax.rem(plane, 2)
    partner_planes = [across_pair, plane + 3 - 2 * corner]
    for i in range(exchanges - 3):
        step = 4 * 2**i
        partner_planes.append(plane + step - 2 * step * lax.rem(plane // step, 2))
    partner_planes.append(across_pair)
    other_nodes = [lax.rem(node + k, nodes) for k in range(1, nodes)]
    other_subs = [flipped(sub, k, subs) for k in range(subs - 1, 0, -1)]
    row0 = node * rows_here
    lower = node < nodes // 2
    own_at = jnp.where(lower, HALO_BLOCKS, 0)

    def fetch(h):
        return pltpu.make_async_copy(
            vectors_hbm.at[:, :, pl.ds(h * wide, wide)],
            padded[h].at[pl.ds(own_at, count)],
            load_sem.at[h],
        )

    tables = [
        pltpu.make_async_copy(source, target, table_sem.at[i])
        for i, (source, target) in enumerate(
            [
                (map_hbm, map_ref), (index_hbm, index_ref),
                (ritz_hbm, ritz_ref), (shift_hbm, shift_ref),
            ]
        )
    ]
    fetch(0).start()
    begin(tables)
    loads = [
        pltpu.make_async_copy(inverses_hbm, inverses, load_sem.at[halves]),
        pltpu.make_async_copy(
            blocks_hbm.at[pl.ds(row0, rows_here)], blocks, load_sem.at[halves + 1]
        ),
        pltpu.make_async_copy(panel_hbm, panel, load_sem.at[halves + 2]),
    ]
    meet(
        [(True, target) for target in near_subs]
        + [(True, {"node": o}) for o in other_nodes]
        + [(sub > 0, {"sub": lax.rem(sub + subs - 1, subs)})]
        + [(sub < subs - 1, {"sub": lax.rem(sub + 1, subs)})]
        + [
            (inside if 0 < i < exchanges - 1 else True, {"sub": partner * inner + place})
            for i, partner in enumerate(partner_planes[:-1])
        ]
    )

    halo_target = {"sub": lax.rem(sub + subs + jnp.where(lower, 1, -1), subs)}
    sends_halo = jnp.where(lower, sub < subs - 1, sub > 0)
    takes_halo = jnp.where(lower, sub > 0, sub < subs - 1)

    def halo(h):
        rows = pl.ds(jnp.where(lower, count - HALO_BLOCKS, 0), HALO_BLOCKS)
        return remote(
            padded[h].at[pl.ds(jnp.where(lower, count, 0), HALO_BLOCKS)],
            padded[h].at[pl.ds(jnp.where(lower, 0, count), HALO_BLOCKS)],
            halo_send.at[h], halo_recv.at[h], halo_target,
        )

    def send_halo(h):
        @pl.when(sends_halo)
        def _():
            halo(h).start()

    fetch(0).wait()
    send_halo(0)
    begin(loads)
    for h in range(1, halves):
        fetch(h).start()
    finish(tables)
    for p in range(sep_blocks):
        value = map_ref[0, p].astype(jnp.float32)
        maps[0, p] = jnp.full(maps.shape[2:], value, jnp.float32)
    tell = [
        remote(maps.at[0], maps.at[k + 1], map_send, map_recv, t)
        for k, t in enumerate(near_subs)
    ]
    begin(tell)

    def constant(values):
        chosen = jnp.float32(values[0])
        for k in range(1, nodes):
            chosen = jnp.where(node == k, jnp.float32(values[k]), chosen)
        return chosen

    angles = [
        [math.pi * (k * node_local + n + 0.5) / total_nodes for k in range(nodes)]
        for n in range(node_local)
    ]
    real_shift = [constant([math.cos(a) for a in row]) for row in angles]
    imag_shift = [constant([math.sin(a) for a in row]) for row in angles]
    real_weight = [constant([2.0 * math.cos(a) / total_nodes for a in row]) for row in angles]
    imag_weight = [constant([2.0 * math.sin(a) / total_nodes for a in row]) for row in angles]

    loads[0].wait()

    def prepare(b, carry):
        for n in range(node_local):
            real, imag = inverses[n, 0, b], inverses[n, 1, b]
            top = 2 * n * size
            inverses_cat[b, top : top + size] = stack_left(real)
            inverses_cat[b, top + size : top + 2 * size] = stack_left(imag)
            hi, lo = split(real_weight[n] * real - imag_weight[n] * imag)
            folds[n, b, :size, :size], folds[n, b, size:, :size] = hi, lo
            hi, lo = split(real_weight[n] * imag + imag_weight[n] * real)
            folds[n, b, :size, size:], folds[n, b, size:, size:] = hi, lo
        return carry

    lax.fori_loop(0, count, prepare, 0)
    loads[1].wait()
    for h in range(1, halves):
        fetch(h).wait()

    def diagonal(i, carry):
        left = stack_left(blocks[i, 0])
        for h in range(halves):
            vectors = padded[h][own_at + row0 + i]
            ritz = ritz_ref[:, h * wide : (h + 1) * wide]
            partial[h, i] = dot(left, stack_right(vectors)) - vectors * ritz
        for q in range(1, blocks.shape[1]):
            blocks_cat[i, :, 3 * size * (q - 1) : 3 * size * q] = stack_left(blocks[i, q])
        return carry

    lax.fori_loop(0, rows_here, diagonal, 0)
    loads[2].wait()
    for p in range(sep_blocks):
        hi, lo = split(panel[p * size : (p + 1) * size])
        panel_hi[p * size : (p + 1) * size] = hi
        panel_lo[p * size : (p + 1) * size] = lo

    for g in range(groups):
        shift_columns[...] = jnp.broadcast_to(shift_ref[g : g + 1, :], (size, size)).T
        for r in range(pieces):
            columns = shift_columns[pl.ds(pl.multiple_of(r * piece_rows + place * span, 8), span), :]
            for n in range(node_local):
                gap = real_shift[n] - columns
                modulus = gap * gap + imag_shift[n] * imag_shift[n]
                by_real[n, r, g] = gap / modulus
                by_imag[n, r, g] = imag_shift[n] / modulus

    strip = size // sep_blocks

    def turn(r, p):
        hi, lo = split(
            jnp.concatenate(
                [
                    panel[q * size + first : q * size + first + span]
                    for first in range(r * piece_rows + p * strip, r * piece_rows + (p + 1) * strip, span)
                    for q in range(sep_blocks)
                ],
                axis=0,
            ).T
        )
        turned_hi[r, :, p * size : (p + 1) * size] = hi
        turned_lo[r, :, p * size : (p + 1) * size] = lo

    def node_copies(h, i):
        return [
            remote(
                residual.at[h, row0 + i], residual.at[h, row0 + i],
                node_send, node_recv.at[k, h, i], {"node": o},
            )
            for k, o in enumerate(other_nodes)
        ]

    def residual_half(h):
        @pl.when(takes_halo)
        def _():
            halo(h).wait_recv()

        if h < halves - 1:
            send_halo(h + 1)

        def step(i, carry):
            rights = []
            for q in range(1, blocks.shape[1]):
                spot = index_ref[q, row0 + i] - sub * count + own_at
                spot = jnp.clip(spot, 0, padded[h].shape[0] - 1)
                rights.append(stack_right(padded[h][spot]))
            total = partial[h, i] + dot(blocks_cat[i], jnp.concatenate(rights, axis=0))
            residual[h, row0 + i] = total
            begin(node_copies(h, i))
            return carry

        lax.fori_loop(0, rows_here, step, 0)

    def guess_half(h):
        def one(b):
            value = dot(inverses_cat[b], stack_right(residual[h, b]))
            hi, lo = split(value)
            for n in range(node_local):
                for c in range(2):
                    rows = slice((2 * n + c) * size, (2 * n + c + 1) * size)
                    k = h * node_local + n
                    guess_hi[k, b, :, c * wide : (c + 1) * wide] = hi[rows]
                    guess_lo[k, b, :, c * wide : (c + 1) * wide] = lo[rows]

        def mine(i, carry):
            one(row0 + i)
            return carry

        lax.fori_loop(0, rows_here, mine, 0)

        def theirs(i, carry):
            for copy in node_copies(h, i):
                copy.wait_recv()
            for k in range(nodes - 1):
                one(lax.rem(node + nodes - 1 - k, nodes) * rows_here + i)
            return carry

        lax.fori_loop(0, rows_here, theirs, 0)

    def rows_of(r, t):
        return pl.ds(pl.multiple_of(r * piece_rows + t * span, 8), span)

    def there_near(j):
        k, r = divmod(j, pieces)
        return [
            remote(
                part.at[k, r, t], near.at[j, i],
                sep_send.at[0], sep_recv.at[j, 0], near_subs[i],
            )
            for i, t in enumerate(near_places)
        ]

    def across(j, i):
        if i == 0:
            source, target = dense.at[j], far.at[j, 0]
        elif i < exchanges - 1:
            source, target = far.at[j, i - 1], far.at[j, i]
        else:
            source, target = coarse.at[j], coarse.at[j]
        return remote(
            source, target, far_send.at[i], far_recv.at[j, i % (exchanges - 1)],
            {"sub": partner_planes[i] * inner + place},
        )

    def home_near(j):
        return [
            remote(
                picked.at[j, i],
                back.at[j, place],
                sep_send.at[1], sep_recv.at[j, 1], near_subs[i],
            )
            for i in range(inner - 1)
        ]

    def stage_a(k):
        rights = (
            guess_hi[k].reshape(count * size, 2 * wide),
            guess_lo[k].reshape(count * size, 2 * wide),
        )
        value = dot_halves((panel_hi[...], panel_lo[...]), rights)
        value = value.reshape(sep_blocks, size, 2 * wide)
        for r in range(pieces):
            for t in range(inner):
                first = r * piece_rows + t * span
                for c in range(2):
                    part[k, r, t, c] = value[:, first : first + span, c * wide : (c + 1) * wide]
            begin(there_near(k * pieces + r))

    def stage_b(j):
        k, r = divmod(j, pieces)
        remote(near.at[j], near.at[j], sep_send.at[0], sep_recv.at[j, 0], near_subs[0]).wait_recv()
        for c in range(2):
            totals = [jnp.zeros((span, wide), jnp.float32) for _ in range(groups)]
            for t in range(inner):
                for p in range(sep_blocks):
                    value = part[k, r, place, c, p] if t == 0 else near[j, t - 1, c, p]
                    here = jnp.broadcast_to(maps[t, p, 0:1], (span, wide))
                    for g in range(groups):
                        totals[g] = totals[g] + jnp.where(here == float(g), value, 0.0)
            for g in range(groups):
                dense[j, c, g] = totals[g]

        @pl.when(jnp.logical_not(inside))
        def _():
            across(j, 0).start()


    def stage_c(j, i):
        k, r = divmod(j, pieces)
        n = k % node_local

        @pl.when(inside)
        def _():
            across(j, i).wait_recv()
            value = far[j, i] + (far[j, i - 1] if i > 0 else dense[j])
            if i < exchanges - 2:
                far[j, i] = value
            else:
                for g in range(groups):
                    scale_real, scale_imag = by_real[n, r, g], by_imag[n, r, g]
                    real, imag = value[0, g], value[1, g]
                    coarse[j, 0, g] = real * scale_real + imag * scale_imag
                    coarse[j, 1, g] = imag * scale_real - real * scale_imag
            across(j, i + 1).start()

    def stage_d(j):
        @pl.when(jnp.logical_not(inside))
        def _():
            across(j, exchanges - 1).wait_recv()

        copies = home_near(j)
        for t in [*range(1, inner), 0]:
            for p in range(sep_blocks):
                here = jnp.broadcast_to(maps[t, p, 0:1], (span, wide))
                for c in range(2):
                    value = coarse[j, c, 0]
                    for g in range(1, groups):
                        value = jnp.where(here == float(g), coarse[j, c, g], value)
                    if t == 0:
                        back[j, place, c, p] = value
                    else:
                        picked[j, t - 1, c, p] = value
            if t > 0:
                copies[t - 1].start()

    share_rows = count // SHARES

    def share_copies(o, k, part):
        rows = pl.ds(part * share_rows, share_rows)
        return remote(
            shares.at[o, rows], landed.at[k, rows], share_send, share_recv.at[k, part], {"node": o}
        )

    def stage_e(j):
        k, r = divmod(j, pieces)
        h, n = divmod(k, node_local)
        come = picked.at[j]
        remote(come, come, sep_send.at[1], sep_recv.at[j, 1], near_subs[0]).wait_recv()
        right = jnp.concatenate(
            [back[j, :, c].reshape(sep_blocks * piece_rows, wide) for c in range(2)], axis=1
        )
        value = dot_halves((turned_hi[r], turned_lo[r]), split(right))
        value = value.reshape(count, size, 2 * wide)
        if r > 0:
            value = value + value_ref[...]
        if r < pieces - 1:
            value_ref[...] = value
            return
        for part in range(SHARES):
            for b in range(part * share_rows, (part + 1) * share_rows):
                below = jnp.concatenate(
                    [residual[h, b] - value[b, :, :wide], value[b, :, wide:]], axis=0
                )
                new = dot(folds[n, b], jnp.concatenate(split(below), axis=1))
                new = new[:size, :wide] + (new[:size, wide:] + new[size:, :wide])
                if n > 0:
                    new = new + weighted[h, b]
                if n < node_local - 1:
                    weighted[h, b] = new
                    continue
                for m in range(per_half):
                    columns = new[:, m * part_cols : (m + 1) * part_cols]
                    shares[h * per_half + m, b] = columns
            if n < node_local - 1:
                continue
            for s, o in enumerate(other_nodes):

                @pl.when(o // per_half == h)
                def _():
                    share_copies(o, s, part).start()

    for r in range(pieces):
        for p in range(sep_blocks // pieces):
            turn(r, p)
    def left(whole, sem):
        remote(whole, whole, sem, sum_recv, near_subs[0]).wait_send()

    def all_left():
        @pl.when(sends_halo)
        def _():
            for h in range(halves):
                halo(h).wait_send()

        left(residual.at[:, pl.ds(0, (nodes - 1) * rows_here)], node_send)
        left(near, sep_send.at[0])

        @pl.when(inside)
        def _():
            for i in range(1, exchanges):
                left(coarse, far_send.at[i])

        @pl.when(jnp.logical_not(inside))
        def _():
            left(coarse, far_send.at[0])

    events = []
    for h in range(halves):
        first = 6.5 * h
        events += [(first - 4.7, residual_half, (h,)), (first - 3.7, guess_half, (h,))]
        for n in range(node_local):
            events.append((first - 1.8 + 1.8 * n, stage_a, (h * node_local + n,)))
    others_maps = maps.at[pl.ds(1, inner - 1)]
    told = remote(others_maps, others_maps, map_send, map_recv, near_subs[0])
    events.append((3.9, finish, ([told],)))
    total_pieces = node_local * halves * pieces
    wire, hop = 2.7, 5.0
    for j in range(total_pieces):
        come = 4.0 + wire * j
        events.append((come, stage_b, (j,)))
        for i in range(exchanges - 1):
            come += hop
            events.append((come, stage_c, (j, i)))
        come += hop
        events.append((come, stage_d, (j,)))
        come = max(come, 1.0 + wire * (total_pieces + j)) + wire + 1.5
        events.append((come, stage_e, (j,)))
    events.append((come - 0.1, all_left, ()))
    for _, stage, which in sorted(events, key=lambda event: event[0]):
        stage(*which)

    def own_vectors(b):
        vectors = padded[0][own_at + b]
        for h in range(1, halves):
            vectors = jnp.where(node // per_half == h, padded[h][own_at + b], vectors)
        chosen = vectors[:, :part_cols]
        for m in range(1, per_half):
            columns = vectors[:, m * part_cols : (m + 1) * part_cols]
            chosen = jnp.where(lax.rem(node, per_half) == m, columns, chosen)
        return chosen

    def update_step(b, squares):
        total = own_vectors(b) - shares[node, b]
        for k in range(nodes - 1):
            total = total - landed[k, b]
        out_ref[b] = total
        return squares + jnp.sum(total * total, axis=0, keepdims=True)

    squares = jnp.zeros((1, part_cols), jnp.float32)
    for part in range(SHARES):
        for k, o in enumerate(other_nodes):
            share_copies(o, k, part).wait_recv()
        first = part * share_rows
        squares = lax.fori_loop(first, first + share_rows, update_step, squares)
    sums[sub] = jnp.broadcast_to(squares, (8, part_cols))
    spread = [
        remote(sums.at[sub], sums.at[sub], sum_send, sum_recv, {"sub": o})
        for o in other_subs
    ]
    begin(spread)

    left(picked, sep_send.at[1])
    left(landed, share_send)
    others_sums = sums.at[pl.ds(0, subs - 1)]
    remote(others_sums, others_sums, sum_send, sum_recv, near_subs[0]).wait()
    total = sums[0]
    for t in range(1, subs):
        total = total + sums[t]
    rows = count * size * subs
    factor_ref[...] = lax.rsqrt(total[0:1] / rows + 1e-06)


def shards(
    search_vectors,
    ritz_values,
    matrix_blocks,
    block_lists,
    inverses,
    panels,
    separator_map,
    separator_shift,
):
    row_count, width = search_vectors.shape
    count, degree, size, _ = matrix_blocks.shape
    nodes, subs = lax.axis_size("node"), lax.axis_size("sub")
    node_local = inverses.shape[0]
    col_count = width // nodes
    vectors = search_vectors.reshape(count, size, width)

    inner = inner_size(subs)
    outer = subs // inner
    sep_blocks = separator_map.shape[1]
    groups = separator_shift.shape[0] // size
    wide = size
    halves = width // wide
    rows_here = count // nodes
    pieces = PIECES
    span = size // pieces // inner
    chunks = node_local * halves
    parts = chunks * pieces
    panel_rows, panel_cols = panels.shape[1:]
    exchanges = 3 + (outer // 4 - 1).bit_length()
    assert subs & (subs - 1) == 0 and inner & (inner - 1) == 0 and count % SHARES == 0
    assert outer == 4 * 2 ** (exchanges - 3)
    assert nodes % 2 == 0 and count % nodes == 0 and 2 * HALO_BLOCKS <= count
    assert nodes % halves == 0 and span % 8 == 0 and size % (sep_blocks * span) == 0 and sep_blocks % pieces == 0
    f32, bf16 = jnp.float32, jnp.bfloat16
    dma = pltpu.SemaphoreType.DMA
    updated, factor = pl.pallas_call(
        functools.partial(kernel, subs, nodes, inner),
        out_shape=[
            jax.ShapeDtypeStruct((count, size, col_count), f32),
            jax.ShapeDtypeStruct((1, col_count), f32),
        ],
        in_specs=[pl.BlockSpec(memory_space=pltpu.HBM)] * 4
        + [pl.BlockSpec(memory_space=pl.ANY)] * 4,
        out_specs=[pl.BlockSpec(memory_space=VMEM)] * 2,
        scratch_shapes=[
            SMEM((degree, count), jnp.int32),
            SMEM(separator_map.shape, jnp.int32),
            VMEM((1, width), f32),
            VMEM((groups, size), f32),
            [VMEM((count + HALO_BLOCKS, size, wide), f32)] * halves,
            VMEM((rows_here, degree, size, size), f32),
            VMEM(inverses.shape, f32),
            VMEM((panel_rows, panel_cols), f32),
            VMEM((size, size), f32),
            VMEM((node_local, pieces, groups, span, wide), f32),
            VMEM((node_local, pieces, groups, span, wide), f32),
            VMEM((inner, sep_blocks, 8, wide), f32),
            VMEM((halves, count, size, wide), f32),
            VMEM((halves, rows_here, size, wide), f32),
            VMEM((rows_here, size, 3 * (degree - 1) * size), bf16),
            VMEM((count, 2 * node_local * size, 3 * size), bf16),
            VMEM((panel_rows, panel_cols), bf16),
            VMEM((panel_rows, panel_cols), bf16),
            VMEM((pieces, panel_cols, panel_rows // pieces), bf16),
            VMEM((pieces, panel_cols, panel_rows // pieces), bf16),
            VMEM((node_local, count, 2 * size, 2 * size), bf16),
            VMEM((chunks, count, size, 2 * wide), bf16),
            VMEM((chunks, count, size, 2 * wide), bf16),
            VMEM((chunks, pieces, inner, 2, sep_blocks, span, wide), f32),
            VMEM((parts, inner - 1, 2, sep_blocks, span, wide), f32),
            VMEM((parts, 2, groups, span, wide), f32),
            VMEM((parts, exchanges - 1, 2, groups, span, wide), f32),
            VMEM((parts, 2, groups, span, wide), f32),
            VMEM((parts, inner - 1, 2, sep_blocks, span, wide), f32),
            VMEM((parts, inner, 2, sep_blocks, span, wide), f32),
            VMEM((count, size, 2 * wide), f32),
            VMEM((halves, count, size, wide), f32),
            VMEM((nodes, count, size, col_count), f32),
            VMEM((nodes - 1, count, size, col_count), f32),
            VMEM((subs, 8, col_count), f32),
            dma((4,)),
            dma((halves + 3,)),
            dma((halves,)),
            dma((halves,)),
            dma,
            dma,
            dma,
            dma((nodes - 1, halves, rows_here)),
            dma((2,)),
            dma((parts, 2)),
            dma((exchanges,)),
            dma((parts, exchanges - 1)),
            dma,
            dma((nodes - 1, SHARES)),
            dma,
            dma,
        ],
        compiler_params=pltpu.CompilerParams(
            collective_id=0, has_side_effects=True, vmem_limit_bytes=54400 * 1024
        ),
        name="update",
    )(
        *(
            pltpu.with_memory_space_constraint(x, pltpu.HBM)
            for x in (
                block_lists.T, separator_map, ritz_values[None],
                separator_shift.reshape(groups, size),
            )
        ),
        vectors, matrix_blocks, inverses, panels[0],
    )
    return (updated * factor[None]).reshape(row_count, col_count)


def solution(mesh):
    return jax.shard_map(
        shards,
        mesh=mesh,
        in_specs=(
            P("sub", None),
            P(),
            P("sub", None, None, None),
            P("sub", None),
            P("node", None, "sub", None, None),
            P("sub", None, None),
            P("sub", None),
            P(),
        ),
        out_specs=P("sub", "node"),
        check_vma=False,
    )
```
